256 devices in a mesh: rows: 32 (over z_lo, y, x), cols: 8 (over z_hi, core).
Axes of the slice: x: 4, y: 4, z: 8 (z_hi: 4, z_lo: 2; z = z_hi * 2 + z_lo), core: 2. Of those that a mesh axis runs over, the one named last changes fastest.
Arguments:
- canvas: bfloat16 [256, 1024, 256], P('rows', 'cols'), may hold values from -16 to 16
- conv_weight: bfloat16 [3, 3, 256, 512], replicated, may hold values from -0.125 to 0.125
- conv_bias: bfloat16 [512], replicated, may hold values from -3 to 3
- target_gram: float32 [512, 512], P(('rows', 'cols')), may hold values from -6 to 6
Outputs:
- gram: float32 [512, 512], P(('rows', 'cols'))
- grad_canvas: bfloat16 [256, 1024, 256], P('rows', 'cols')
The draws below stay inside these ranges and needn't reach their ends.
All inputs are finite; a program needn't handle non-finite values.
Results may differ from the reference program's by a relative error of at most 0.009.
Values may be sent and summed in bfloat16 or wider, within the bound.
A program may use at most 64 MiB of HBM per device.

```python
import math
import jax
import jax.numpy as jnp
from jax import lax

CI = 256
CO = 512
TR = 8
TC = 128
H = 256
W = 1024
NPIX = 262144
N_ROWS = 32


def draw_canvas(key, part):
    key_base = jax.random.fold_in(key, 11)
    key_rough = jax.random.fold_in(key, 12)
    key_chan = jax.random.fold_in(key, 13)
    key_heavy = jax.random.fold_in(key, 15)
    row_place = jnp.arange(H, dtype=jnp.float32) / H
    rough = jax.random.uniform(key_rough, (H, 1, 1), jnp.float32, -0.6, 0.6)
    row_scale = jnp.exp(0.55 * (2.0 * row_place[:, None, None] - 1.0) + rough)
    chan_scale = jnp.exp(jax.random.uniform(key_chan, (1, 1, CI), jnp.float32, -0.5, 0.5))
    band_count = H // TR
    strip_count = W // TC
    heavy_strip = jax.random.randint(key_heavy, (band_count,), 0, strip_count)
    band_of_row = jnp.arange(H, dtype=jnp.int32) // TR
    strip_of_col = jnp.arange(W, dtype=jnp.int32) // TC
    chosen = heavy_strip[band_of_row]
    heavy = (band_of_row[:, None] % 4 == 0) & (strip_of_col[None, :] == chosen[:, None])
    heavy_scale = jnp.where(heavy, 4.0, 1.0).astype(jnp.float32)[:, :, None]
    base = jax.random.normal(key_base, (H, W, CI), jnp.float32)
    return jnp.clip(base * row_scale * chan_scale * heavy_scale, -16.0, 16.0).astype(jnp.bfloat16)


def level_of(rng, dims, split, low, largest):
    def one(position, blocks):
        draws = jax.random.uniform(jax.random.fold_in(jax.random.fold_in(rng, 6), position), (blocks,), jnp.float32, low / len(split), largest / len(split))
        return jnp.repeat(jnp.exp(draws), dims[position] // blocks).reshape((-1,) + (1,) * (len(dims) - position - 1))

    gain = one(*split[0])
    for cut in split[1:]:
        gain = gain * one(*cut)
    return gain


def scatter_about(key, dims, deviation, most, split=(), kind=jnp.bfloat16):
    entries = jax.random.normal(key, dims, jnp.float32) * deviation
    if len(split) > 0:
        entries = level_of(key, dims, split, -0.22, 0.18) * entries
    return jnp.clip(entries, min=-most, max=most).astype(kind)


def setup_inputs(seed: int = 0) -> dict:
    seeds = jax.random.split(jax.random.key(seed), 5)
    return {
        "canvas": draw_canvas(jax.random.fold_in(seeds[4], 71), 0),
        "conv_weight": scatter_about(seeds[1], (3, 3, CI, CO), (9 * CI) ** -0.5, 0.125),
        "conv_bias": scatter_about(seeds[2], (CO,), 0.5, 3.0),
        "target_gram": scatter_about(seeds[3], (CO, CO), 1.0, 6.0, ((0, 256),), jnp.float32),
    }


gelu_scale = math.sqrt(2.0 / math.pi)

def gelu_grad(value):
    tangent = jnp.tanh(gelu_scale * (value + 0.044715 * value * value * value))
    return 0.5 * (1.0 + tangent) + 0.5 * value * (1.0 - tangent * tangent) * gelu_scale * (1.0 + 3.0 * 0.044715 * value * value)

def patches(padded, tile_rows, tile_cols):
    pieces = [padded[row_off:row_off + tile_rows, col_off:col_off + tile_cols, :] for row_off in range(3) for col_off in range(3)]
    return jnp.concatenate(pieces, axis=2).reshape(tile_rows * tile_cols, -1)

def reference(canvas, conv_weight, conv_bias, target_gram):
    padded = jnp.pad(canvas, ((1, 1), (1, 1), (0, 0)))
    kernel = conv_weight.reshape(9 * CI, CO)
    flipped = conv_weight[::-1, ::-1].transpose(0, 1, 3, 2).reshape(9 * CO, CI)
    bands = jnp.arange(N_ROWS, dtype=jnp.int32)

    def preact_band(band_index):
        begin = (band_index * TR).astype(jnp.int32)
        window = lax.dynamic_slice_in_dim(padded, begin, TR + 2, 0)
        return jnp.dot(patches(window, TR, W), kernel, preferred_element_type=jnp.float32) + conv_bias.astype(jnp.float32)

    def feature_band(band_index):
        return jax.nn.gelu(preact_band(band_index), approximate=True).astype(jnp.bfloat16)
    features = lax.map(feature_band, bands).reshape(H * W, CO)
    gram = lax.dot_general(features, features, (((0,), (0,)), ((), ())), preferred_element_type=jnp.float32) / NPIX
    error = gram - target_gram
    symmetric = (error + error.T).astype(jnp.bfloat16)

    def grad_band(band_index):
        preact = preact_band(band_index)
        begin = (band_index * TR * W).astype(jnp.int32)
        own_rows = lax.dynamic_slice_in_dim(features, begin, TR * W, 0)
        upstream = jnp.dot(own_rows, symmetric, preferred_element_type=jnp.float32) / math.sqrt(CO)
        return (upstream * gelu_grad(preact)).astype(jnp.bfloat16)
    grad_pre = lax.map(grad_band, bands).reshape(H, W, CO)
    grad_padded = jnp.pad(grad_pre, ((1, 1), (1, 1), (0, 0)))

    def input_band(band_index):
        begin = (band_index * TR).astype(jnp.int32)
        window = lax.dynamic_slice_in_dim(grad_padded, begin, TR + 2, 0)
        return jnp.dot(patches(window, TR, W), flipped, preferred_element_type=jnp.float32).astype(jnp.bfloat16)
    grad_canvas = lax.map(input_band, bands).reshape(H, W, CI)
    return (gram, grad_canvas)
```

```python
import math

import jax
import jax.numpy as jnp
from jax import lax
from jax.experimental import pallas as pl
from jax.experimental.pallas import tpu as pltpu
from jax.sharding import PartitionSpec as P

MESH = pl.DeviceIdType.MESH
f32, bf16 = jnp.float32, jnp.bfloat16
C0 = math.sqrt(2.0 / math.pi)
C1 = C0 * 0.044715
TR, TC, CI, CO = 8, 128, 256, 512
NPIX = 262144
NR, NC = 32, 8
RING = 10 * TC


def gelu_pair(v):
    square = v * v
    half = 0.5 + 0.5 * jnp.tanh(v * (C0 + C1 * square))
    feat = v * half
    slope = half + feat * (1.0 - half) * (2.0 * C0 + 6.0 * C1 * square)
    return feat, slope


def kernel(
    canvas, weight, bias, target, gram_out, grad_out,
    xs, left, right, wv, feats, deriv, gp, gring, ringx, pan, s0, r0, s1, r1, s2, r2, gf,
    sym, tt, gfull, t2, tz, tc, tb, outv, outg, edge,
    lsem, hsend, hrecv, send, xrecv, zrecv, arecv, frecv, srecv, tsrecv, tzrecv, txrecv, tfrecv, osem,
):
    r = lax.axis_index("rows")
    c = lax.axis_index("cols")
    xy, zl, core, zh = r % 16, r // 16, c % 2, c // 2
    z = zh * 2 + zl
    sib = (r, c + 1 - 2 * core)

    def xyp(j):
        return (zl * 16 + (xy + j) % 16, c)

    def zp(j):
        z2 = (z + j) % 8
        return ((z2 % 2) * 16 + xy, (z2 // 2) * 2 + core)

    def rcopy(src, dst, ssem, rsem, dev):
        return pltpu.make_async_remote_copy(
            src_ref=src, dst_ref=dst, send_sem=ssem, recv_sem=rsem, device_id=dev, device_id_type=MESH
        )

    ld_canvas = pltpu.make_async_copy(canvas, xs.at[1, pl.ds(2, TR)], lsem.at[0])
    ld_weight = pltpu.make_async_copy(weight, wv, lsem.at[1])
    ld_target = pltpu.make_async_copy(target, t2.at[core], lsem.at[2])
    ld_canvas.start()
    ld_weight.start()
    ld_target.start()

    has_up, has_dn, has_lf, has_rt = r > 0, r < NR - 1, c > 0, c < NC - 1
    halo = []
    for dr in (-1, 0, 1):
        for dc in (-1, 0, 1):
            if dr == 0 and dc == 0:
                continue
            cond = None
            for step, flag in ((dr, (has_up, has_dn)), (dc, (has_lf, has_rt))):
                if step:
                    this = flag[0] if step < 0 else flag[1]
                    cond = this if cond is None else jnp.logical_and(cond, this)
            halo.append((dr, dc, cond))
    bar = pltpu.get_barrier_semaphore()
    count = jnp.int32(23)
    for dr, dc, cond in halo:
        count = count + jnp.where(cond, 1, 0)

        @pl.when(cond)
        def _():
            pl.semaphore_signal(bar, inc=1, device_id=(r + dr, c + dc), device_id_type=MESH)

    pl.semaphore_signal(bar, inc=1, device_id=sib, device_id_type=MESH)
    for j in range(1, 16):
        pl.semaphore_signal(bar, inc=1, device_id=xyp(j), device_id_type=MESH)
    for j in range(1, 8):
        pl.semaphore_signal(bar, inc=1, device_id=zp(j), device_id_type=MESH)
    pl.semaphore_wait(bar, count)

    def halo_copy(k, dr, dc):
        rows_src = pl.ds(0, 2) if dr < 0 else (pl.ds(TR - 2, 2) if dr > 0 else pl.ds(0, TR))
        rows_dst = pl.ds(TR + 2, 2) if dr < 0 else (pl.ds(0, 2) if dr > 0 else pl.ds(2, TR))
        if dc == 0:
            src, dst = canvas.at[rows_src], xs.at[1, rows_dst]
        elif dc < 0:
            src, dst = canvas.at[rows_src, pl.ds(0, 8)], right.at[rows_dst]
        else:
            src, dst = canvas.at[rows_src, pl.ds(TC - 8, 8)], left.at[rows_dst]
        return rcopy(src, dst, hsend.at[k], hrecv.at[k], (r + dr, c + dc))

    for k, (dr, dc, cond) in enumerate(halo):

        @pl.when(cond)
        def _():
            halo_copy(k, dr, dc).start()

    t_sib = rcopy(target, t2.at[core], send.at[0], tsrecv, sib)
    t_sib.start()

    @pl.when(r == 0)
    def _():
        xs[1, 0:2] = jnp.zeros((2, TC, CI), bf16)
        left[0:2] = jnp.zeros((2, 8, CI), bf16)
        right[0:2] = jnp.zeros((2, 8, CI), bf16)

    @pl.when(r == NR - 1)
    def _():
        xs[1, TR + 2 : TR + 4] = jnp.zeros((2, TC, CI), bf16)
        left[TR + 2 : TR + 4] = jnp.zeros((2, 8, CI), bf16)
        right[TR + 2 : TR + 4] = jnp.zeros((2, 8, CI), bf16)

    @pl.when(c == 0)
    def _():
        left[...] = jnp.zeros((TR + 4, 8, CI), bf16)

    @pl.when(c == NC - 1)
    def _():
        right[...] = jnp.zeros((TR + 4, 8, CI), bf16)

    ld_canvas.wait()
    ld_target.wait()
    for k, (dr, dc, cond) in enumerate(halo):

        @pl.when(cond)
        def _():
            halo_copy(7 - k, -dr, -dc).wait_recv()

    t_sib.wait_recv()
    quads = []
    for b in range(2):
        for q in range(2):
            rows2 = t2[q]
            quads.append(
                jnp.where(core == 0, rows2[:, b * 128 : b * 128 + 128], rows2[:, 256 + b * 128 : 384 + b * 128])
            )
    tz[z] = jnp.concatenate(quads, axis=0)
    t_z = [rcopy(tz.at[z], tz.at[z], send.at[j], tzrecv.at[j], zp(j)) for j in range(1, 8)]
    for cp in t_z:
        cp.start()

    lane_row = lax.broadcasted_iota(jnp.int32, (TC, CI), 0)

    def shift_row(i, carry):
        row = xs[1, i].astype(f32)
        lcol = left[i].astype(f32)[7:8]
        rcol = right[i].astype(f32)[0:1]
        xs[0, i] = jnp.where(lane_row == 0, lcol, pltpu.roll(row, 1, axis=0)).astype(bf16)
        xs[2, i] = jnp.where(lane_row == TC - 1, rcol, pltpu.roll(row, TC - 1, axis=0)).astype(bf16)
        return carry

    lax.fori_loop(0, TR + 4, shift_row, 0)
    ld_weight.wait()
    bias_row = bias[...].astype(f32).reshape(1, CO)
    wflat = wv.reshape(9 * CI, CO)

    def conv(parts):
        lhs = jnp.concatenate(parts, axis=1)
        return jnp.dot(lhs, wflat[...], preferred_element_type=f32) + bias_row

    def emit(start, v, scale):
        feat, slope = gelu_pair(v)
        feats[pl.ds(start, v.shape[0])] = feat.astype(bf16)
        deriv[pl.ds(start, v.shape[0])] = slope * scale
        return feat.astype(bf16)

    scale = 1.0 / math.sqrt(CO)
    pan[...] = jnp.zeros(pan.shape, f32)

    def main_tile(t, carry):
        h = 2 * t
        parts = [xs[b, pl.ds(h + a + 1, 2)].reshape(2 * TC, CI) for a in range(3) for b in range(3)]
        feat = emit(pl.multiple_of((h + 1) * TC, TC), conv(parts), scale)
        lo, hi = feat[:, 0:256], feat[:, 256:512]
        for q, (one, two) in enumerate(((lo, lo), (lo, hi), (hi, hi))):
            prod = lax.dot_general(one, two, (((0,), (0,)), ((), ())), preferred_element_type=f32)
            for s in range(2):
                at = (2 * q + s) * 256
                pan[at : at + 256] = pan[at : at + 256] + prod[:, s * 128 : s * 128 + 128]
        return carry

    lax.fori_loop(0, TR // 2, main_tile, 0)

    own_half = pl.multiple_of(core * 768, 768)
    other_half = pl.multiple_of((1 - core) * 768, 768)
    s0[...] = pan[pl.ds(other_half, 768)].astype(bf16)
    g_sib = rcopy(s0, r0, send.at[8], srecv, sib)
    g_sib.start()
    for cp in t_z:
        cp.wait_recv()
    for zz in range(2):
        for b in range(2):
            rows16 = jnp.concatenate([tz[q * 2 + zz][b * 4 : b * 4 + 4] for q in range(4)], axis=0)
            tc[(zz * 2 + b) * 16 : (zz * 2 + b) * 16 + 16] = rows16.astype(bf16)
    g_sib.wait_recv()
    half = pan[pl.ds(own_half, 768)] + r0[...].astype(f32)
    s1[...] = half.astype(bf16)
    pan[pl.ds(own_half, 768)] = half

    g_xy = []
    for j in range(1, 16):
        k = (xy + j) % 16
        g_xy.append(
            rcopy(s1.at[pl.ds(pl.multiple_of(48 * k, 16), 48)], r1.at[j], send.at[8 + j], xrecv.at[j], xyp(j))
        )
    for cp in g_xy:
        cp.start()
    own_t = tb.at[core, pl.ds(pl.multiple_of(64 * xy, 64), 64)]
    t_xy = [rcopy(tc, own_t, send.at[23 + j], txrecv.at[j], xyp(j)) for j in range(1, 16)]
    for cp in t_xy:
        cp.start()
    tb[core, pl.ds(pl.multiple_of(64 * xy, 64), 64)] = tc[...]

    up_on = jnp.where(has_up, scale, 0.0).astype(f32)
    dn_on = jnp.where(has_dn, scale, 0.0).astype(f32)
    lf_on = jnp.where(has_lf, 1.0, 0.0).astype(f32)
    rt_on = jnp.where(has_rt, 1.0, 0.0).astype(f32)
    emit(0, conv([xs[b, a] for a in range(3) for b in range(3)]), up_on)
    emit(9 * TC, conv([xs[b, 9 + a] for a in range(3) for b in range(3)]), dn_on)
    ringx[...] = jnp.zeros(ringx.shape, f32)
    lcols = left[...].astype(f32)
    rcols = right[...].astype(f32)
    first = xs[1, :, 0:8].astype(f32)
    last = xs[1, :, TC - 8 : TC].astype(f32)
    sides = ((lcols[:, 6], lcols[:, 7], first[:, 0]), (last[:, 7], rcols[:, 0], rcols[:, 1]))
    for s, cols in enumerate(sides):
        for b in range(3):
            for a in range(3):
                k = (a * 3 + b) * CI
                ringx[16 * s : 16 * s + 10, k : k + CI] = cols[b][a : a + 10]
    ring_row = lax.broadcasted_iota(jnp.int32, (32, CO), 0)
    side_on = jnp.where(ring_row < 16, lf_on, rt_on)
    pos = ring_row % 16
    row_on = jnp.where(pos == 0, up_on, jnp.where(pos == 9, dn_on, jnp.where(pos < 9, scale, 0.0)))
    emit(RING, conv([ringx[...].astype(bf16)]), side_on * row_on)

    own48 = pl.multiple_of(own_half + 48 * xy, 16)
    acc = pan[pl.ds(own48, 48)]
    for j in range(1, 16):
        g_xy[j - 1].wait_recv()
        acc = acc + r1[j].astype(f32)
    s2[...] = acc.astype(bf16)

    g_z = [rcopy(s2, r2.at[j], send.at[38 + j], zrecv.at[j], zp(j)) for j in range(1, 8)]
    for cp in g_z:
        cp.start()
    for cp in t_xy:
        cp.wait_recv()
    t_fw = rcopy(tb.at[core], tb.at[core], send.at[46], tfrecv, sib)
    t_fw.start()
    acc = s2[...].astype(f32)
    for j in range(1, 8):
        g_z[j - 1].wait_recv()
        acc = acc + r2[j].astype(f32)
    gf[pl.ds(own48, 48)] = (acc * (1.0 / NPIX)).astype(bf16)

    own_g = gf.at[pl.ds(own48, 48)]
    g_ag = [rcopy(own_g, own_g, send.at[46 + j], arecv.at[j], xyp(j)) for j in range(1, 16)]
    for cp in g_ag:
        cp.start()

    t_fw.wait_recv()

    def tquad(i, k):
        halves = []
        for q in range(2):
            blk = tb[k].reshape(16, 4, 16, 128)[:, i * 2 + q].reshape(256, 128)
            halves.append(blk.astype(f32))
        return jnp.concatenate(halves, axis=1)

    t01 = tquad(0, 1) + tquad(1, 0).T
    t00 = tquad(0, 0)
    t11 = tquad(1, 1)
    tt[0] = t00 + t00.T
    tt[1] = t01
    tt[2] = t01.T
    tt[3] = t11 + t11.T

    for cp in g_ag:
        cp.wait_recv()
    half_g = gf.at[pl.ds(own_half, 768)]
    g_fw = rcopy(half_g, half_g, send.at[62], frecv, sib)
    g_fw.start()
    g_fw.wait_recv()

    def gquad(q):
        return jnp.concatenate([gf[q * 512 : q * 512 + 256], gf[q * 512 + 256 : q * 512 + 512]], axis=1).astype(f32)

    g00, g01, g11 = gquad(0), gquad(1), gquad(2)
    g10 = g01.T
    sym[0:256, 0:256] = (2.0 * g00 - tt[0]).astype(bf16)
    sym[0:256, 256:512] = (2.0 * g01 - tt[1]).astype(bf16)
    sym[256:512, 0:256] = (2.0 * g10 - tt[2]).astype(bf16)
    sym[256:512, 256:512] = (2.0 * g11 - tt[3]).astype(bf16)
    gfull[0:256, 0:256] = g00
    gfull[0:256, 256:512] = g01
    gfull[256:512, 0:256] = g10
    gfull[256:512, 256:512] = g11

    def grad_tile(t, carry):
        at = pl.multiple_of(t * 256, 256)
        up = jnp.dot(feats[pl.ds(at, 256)], sym[...], preferred_element_type=f32)
        gp[pl.ds(at, 256)] = (up * deriv[pl.ds(at, 256)]).astype(bf16)
        return carry

    lax.fori_loop(0, 5, grad_tile, 0)
    upr = jnp.dot(feats[RING : RING + 32], sym[...], preferred_element_type=f32)
    gring[...] = (upr * deriv[RING : RING + 32]).astype(bf16).astype(f32)

    nt = (((1,), (1,)), ((), ()))
    for s, b in ((0, 2), (1, 0)):
        total = jnp.zeros((8, CI), f32)
        for a in range(3):
            rows8 = gring[16 * s + 2 - a : 16 * s + 10 - a].astype(bf16)
            total = total + lax.dot_general(rows8, wv[a * 3 + b], nt, preferred_element_type=f32)
        for h in range(TR):
            edge[s, h] = total[h : h + 1]

    def out_tile(t, carry):
        h = 2 * t
        total = jnp.zeros((2 * TC, 3 * CI), f32)
        for a in range(3):
            at = pl.multiple_of((h + 2 - a) * TC, TC)
            total = total + lax.dot_general(
                gp[pl.ds(at, 2 * TC)], wv[3 * a : 3 * a + 3].reshape(3 * CI, CO), nt, preferred_element_type=f32
            )
        for i in range(2):
            rows = total[i * TC : (i + 1) * TC]
            p0 = jnp.where(lane_row == TC - 1, edge[1, h + i], pltpu.roll(rows[:, 0:CI], TC - 1, axis=0))
            p2 = jnp.where(lane_row == 0, edge[0, h + i], pltpu.roll(rows[:, 2 * CI :], 1, axis=0))
            outv[h + i] = (rows[:, CI : 2 * CI] + p0 + p2).astype(bf16)
        pltpu.make_async_copy(outv.at[pl.ds(h, 2)], grad_out.at[pl.ds(h, 2)], osem.at[t]).start()
        return carry

    lax.fori_loop(0, TR // 2, out_tile, 0)

    own_row = zl * 256 + xy * 16 + zh * 4 + core * 2
    rows8 = gfull[pl.ds(pl.multiple_of((own_row // 8) * 8, 8), 8)]
    sub = lax.broadcasted_iota(jnp.int32, (8, CO), 0)
    for k in range(2):
        outg[k : k + 1] = jnp.sum(jnp.where(sub == own_row % 8 + k, rows8, 0.0), axis=0, keepdims=True)
    g_out = pltpu.make_async_copy(outg, gram_out, osem.at[4])
    g_out.start()
    g_out.wait()
    for t in range(TR // 2):
        pltpu.make_async_copy(outv.at[pl.ds(2 * t, 2)], grad_out.at[pl.ds(2 * t, 2)], osem.at[t]).wait()
    for k, (dr, dc, cond) in enumerate(halo):

        @pl.when(cond)
        def _():
            halo_copy(k, dr, dc).wait_send()

    for cp in [t_sib, g_sib, t_fw, g_fw] + t_z + g_xy + t_xy + g_z + g_ag:
        cp.wait_send()


def on_device(canvas, conv_weight, conv_bias, target_gram):
    hbm = pl.BlockSpec(memory_space=pl.ANY)
    vmem = pl.BlockSpec(memory_space=pltpu.VMEM)
    dma = pltpu.SemaphoreType.DMA
    return pl.pallas_call(
        kernel,
        out_shape=(jax.ShapeDtypeStruct((2, CO), f32), jax.ShapeDtypeStruct((TR, TC, CI), bf16)),
        in_specs=[hbm, hbm, vmem, hbm],
        out_specs=(hbm, hbm),
        scratch_shapes=[
            pltpu.VMEM((3, TR + 4, TC, CI), bf16),
            pltpu.VMEM((TR + 4, 8, CI), bf16),
            pltpu.VMEM((TR + 4, 8, CI), bf16),
            pltpu.VMEM((9, CI, CO), bf16),
            pltpu.VMEM((RING + 32, CO), bf16),
            pltpu.VMEM((RING + 32, CO), f32),
            pltpu.VMEM((RING, CO), bf16),
            pltpu.VMEM((32, CO), f32),
            pltpu.VMEM((32, 9 * CI), f32),
            pltpu.VMEM((1536, 128), f32),
            pltpu.VMEM((768, 128), bf16),
            pltpu.VMEM((768, 128), bf16),
            pltpu.VMEM((768, 128), bf16),
            pltpu.VMEM((16, 48, 128), bf16),
            pltpu.VMEM((48, 128), bf16),
            pltpu.VMEM((8, 48, 128), bf16),
            pltpu.VMEM((1536, 128), bf16),
            pltpu.VMEM((CO, CO), bf16),
            pltpu.VMEM((4, 256, 256), f32),
            pltpu.VMEM((CO, CO), f32),
            pltpu.VMEM((2, 2, CO), f32),
            pltpu.VMEM((8, 8, 128), f32),
            pltpu.VMEM((64, 128), bf16),
            pltpu.VMEM((2, 1024, 128), bf16),
            pltpu.VMEM((TR, TC, CI), bf16),
            pltpu.VMEM((2, CO), f32),
            pltpu.VMEM((2, TR, 1, CI), f32),
            dma((3,)),
            dma((8,)),
            dma((8,)),
            dma((63,)),
            dma((16,)),
            dma((8,)),
            dma((16,)),
            dma,
            dma,
            dma,
            dma((8,)),
            dma((16,)),
            dma,
            dma((5,)),
        ],
        compiler_params=pltpu.CompilerParams(
            collective_id=0, has_side_effects=True, vmem_limit_bytes=56 * 1024 * 1024
        ),
        name="style_grad",
    )(canvas, conv_weight.reshape(9, CI, CO), conv_bias, target_gram)


def solution(mesh):
    return jax.shard_map(
        on_device,
        mesh=mesh,
        in_specs=(P("rows", "cols", None), P(), P(), P(("rows", "cols"), None)),
        out_specs=(P(("rows", "cols"), None), P("rows", "cols", None)),
        check_vma=False,
    )
```

```python
import math

import jax
import jax.numpy as jnp
from jax import lax
from jax.experimental import pallas as pl
from jax.experimental.pallas import tpu as pltpu
from jax.sharding import PartitionSpec as P

MESH = pl.DeviceIdType.MESH
f32, bf16 = jnp.float32, jnp.bfloat16
C0 = math.sqrt(2.0 / math.pi)
C1 = C0 * 0.044715
TR, TC, CI, CO = 8, 128, 256, 512
NPIX = 262144
NR, NC = 32, 8
RING = 10 * TC
XY_STEPS = sorted(
    ((i, j) for i in range(4) for j in range(4) if i or j), key=lambda s: (-min(s[0], 4 - s[0]) - min(s[1], 4 - s[1]), s)
)
Z_STEPS = (4, 3, 5, 2, 6, 1, 7)


def gelu_pair(v):
    square = v * v
    half = 0.5 + 0.5 * jnp.tanh(v * (C0 + C1 * square))
    feat = v * half
    slope = half + feat * (1.0 - half) * (2.0 * C0 + 6.0 * C1 * square)
    return feat, slope


def kernel(
    canvas, weight, bias, target, gram_out, grad_out,
    xs, left, right, wv, wt, feats, deriv, gp, gring, ringx, edgex, pan, s0, r0, s1, r1, s2, r2, gf,
    sym, tt, gfull, t2, tz, tc, tb, outv, outg, edge,
    lsem, hsend, hrecv, send, xrecv, zrecv, arecv, frecv, srecv, tsrecv, tzrecv, txrecv, tfrecv, osem,
):
    r = lax.axis_index("rows")
    c = lax.axis_index("cols")
    xy, zl, core, zh = r % 16, r // 16, c % 2, c // 2
    z = zh * 2 + zl
    sib = (r, c + 1 - 2 * core)

    x, y = xy % 4, xy // 4

    def xyk(j, sign=1):
        dx, dy = XY_STEPS[j - 1]
        return (x + sign * dx + 4) % 4 + 4 * ((y + sign * dy + 4) % 4)

    def xyp(j):
        return (zl * 16 + xyk(j), c)

    def zp(j):
        z2 = (z + Z_STEPS[j - 1]) % 8
        return ((z2 % 2) * 16 + xy, (z2 // 2) * 2 + core)

    def rcopy(src, dst, ssem, rsem, dev):
        return pltpu.make_async_remote_copy(
            src_ref=src, dst_ref=dst, send_sem=ssem, recv_sem=rsem, device_id=dev, device_id_type=MESH
        )

    ld_canvas = pltpu.make_async_copy(canvas, xs.at[1, pl.ds(2, TR)], lsem.at[0])
    ld_weight = pltpu.make_async_copy(weight, wv, lsem.at[1])
    ld_target = pltpu.make_async_copy(target, t2.at[core], lsem.at[2])
    ld_canvas.start()
    ld_weight.start()
    ld_target.start()

    has_up, has_dn, has_lf, has_rt = r > 0, r < NR - 1, c > 0, c < NC - 1
    halo = []
    for dr in (-1, 0, 1):
        for dc in (-1, 0, 1):
            if dr == 0 and dc == 0:
                continue
            cond = None
            for step, flag in ((dr, (has_up, has_dn)), (dc, (has_lf, has_rt))):
                if step:
                    this = flag[0] if step < 0 else flag[1]
                    cond = this if cond is None else jnp.logical_and(cond, this)
            halo.append((dr, dc, cond))
    bar = pltpu.get_barrier_semaphore()
    count = jnp.int32(23)
    for dr, dc, cond in halo:
        count = count + jnp.where(cond, 1, 0)

        @pl.when(cond)
        def _():
            pl.semaphore_signal(bar, inc=1, device_id=(r + dr, c + dc), device_id_type=MESH)

    pl.semaphore_signal(bar, inc=1, device_id=sib, device_id_type=MESH)
    for j in range(1, 16):
        pl.semaphore_signal(bar, inc=1, device_id=xyp(j), device_id_type=MESH)
    for j in range(1, 8):
        pl.semaphore_signal(bar, inc=1, device_id=zp(j), device_id_type=MESH)
    pl.semaphore_wait(bar, count)

    kinds = [(dr, dc, 0) for dr, dc, _ in halo]
    kinds = [(-1, 0, 0), (1, 0, 0)] + [k for k in kinds if k[1]] + [(-1, 0, 1), (1, 0, 1)]
    flags = {(dr, dc): cond for dr, dc, cond in halo}

    def halo_copy(dr, dc, outer):
        k = kinds.index((dr, dc, outer))
        if dc == 0:
            src = canvas.at[outer] if dr < 0 else canvas.at[TR - 1 - outer]
            dst = xs.at[1, TR + 2 + outer] if dr < 0 else xs.at[1, 1 - outer]
        else:
            rows_src = pl.ds(0, 2) if dr < 0 else (pl.ds(TR - 2, 2) if dr > 0 else pl.ds(0, TR))
            rows_dst = pl.ds(TR + 2, 2) if dr < 0 else (pl.ds(0, 2) if dr > 0 else pl.ds(2, TR))
            if dc < 0:
                src, dst = canvas.at[rows_src, pl.ds(0, 8)], right.at[rows_dst]
            else:
                src, dst = canvas.at[rows_src, pl.ds(TC - 8, 8)], left.at[rows_dst]
        return rcopy(src, dst, hsend.at[k], hrecv.at[k], (r + dr, c + dc))

    def each_halo(some, act):
        for dr, dc, outer in some:

            @pl.when(flags[dr, dc])
            def _():
                act(dr, dc, outer)

    each_halo(kinds, lambda dr, dc, outer: halo_copy(dr, dc, outer).start())

    t_sib = rcopy(target, t2.at[core], send.at[0], tsrecv, sib)
    t_sib.start()

    @pl.when(r == 0)
    def _():
        xs[1, 0:2] = jnp.zeros((2, TC, CI), bf16)
        left[0:2] = jnp.zeros((2, 8, CI), bf16)
        right[0:2] = jnp.zeros((2, 8, CI), bf16)

    @pl.when(r == NR - 1)
    def _():
        xs[1, TR + 2 : TR + 4] = jnp.zeros((2, TC, CI), bf16)
        left[TR + 2 : TR + 4] = jnp.zeros((2, 8, CI), bf16)
        right[TR + 2 : TR + 4] = jnp.zeros((2, 8, CI), bf16)

    @pl.when(c == 0)
    def _():
        left[...] = jnp.zeros((TR + 4, 8, CI), bf16)

    @pl.when(c == NC - 1)
    def _():
        right[...] = jnp.zeros((TR + 4, 8, CI), bf16)

    lane_row = lax.broadcasted_iota(jnp.int32, (TC, CI), 0)

    def shift_row(i):
        row = xs[1, i].astype(f32)
        xs[0, i] = pltpu.roll(row, 1, axis=0).astype(bf16)
        xs[2, i] = pltpu.roll(row, TC - 1, axis=0).astype(bf16)

    def shift_edges(i):
        sub = lax.broadcasted_iota(jnp.int32, (16, CI), 0)
        top = xs[0, i, 0:16].astype(f32)
        xs[0, i, 0:16] = jnp.where(sub == 0, left[i].astype(f32)[7:8], top).astype(bf16)
        bot = xs[2, i, TC - 16 : TC].astype(f32)
        xs[2, i, TC - 16 : TC] = jnp.where(sub == 15, right[i].astype(f32)[0:1], bot).astype(bf16)

    ld_canvas.wait()

    def shift_own(i, carry):
        shift_row(i + 2)
        return carry

    lax.fori_loop(0, TR, shift_own, 0)
    ld_weight.wait()
    bias_row = bias[...].astype(f32).reshape(1, CO)
    wflat = wv.reshape(9 * CI, CO)

    def conv(parts):
        lhs = jnp.concatenate(parts, axis=1)
        return jnp.dot(lhs, wflat[...], preferred_element_type=f32) + bias_row

    def taps(h, n):
        return [xs[b, h + a + 1 : h + a + 1 + n].reshape(n * TC, CI) for a in range(3) for b in range(3)]

    scale = 1.0 / math.sqrt(CO)

    def add_gram(feat, fresh):
        lo, hi = feat[:, 0:256], feat[:, 256:512]
        for q, (one, two) in enumerate(((lo, lo), (lo, hi), (hi, hi))):
            prod = lax.dot_general(one, two, (((0,), (0,)), ((), ())), preferred_element_type=f32)
            for s in range(2):
                at = (2 * q + s) * 256
                part = prod[:, s * 128 : s * 128 + 128]
                pan[at : at + 256] = part if fresh else pan[at : at + 256] + part

    feat, slope = gelu_pair(conv(taps(1, 6)))
    feats[2 * TC : 8 * TC] = feat.astype(bf16)
    deriv[2 * TC : 8 * TC] = slope * scale
    sub16 = lax.broadcasted_iota(jnp.int32, (16, CO), 0)

    def put_row(ref, at, place, row):
        old = ref[at : at + 16].astype(f32)
        ref[at : at + 16] = jnp.where(sub16 == place, row, old).astype(ref.dtype)

    for h in range(1, 7):
        put_row(feats, (h + 1) * TC, 0, 0.0)
        put_row(feats, (h + 2) * TC - 16, 15, 0.0)
    add_gram(feats[2 * TC : 8 * TC], True)

    ld_target.wait()
    t_sib.wait_recv()
    quads = []
    for b in range(2):
        for q in range(2):
            rows2 = t2[q]
            quads.append(
                jnp.where(core == 0, rows2[:, b * 128 : b * 128 + 128], rows2[:, 256 + b * 128 : 384 + b * 128])
            )
    tz[z] = jnp.concatenate(quads, axis=0)
    t_z = [rcopy(tz.at[z], tz.at[z], send.at[j], tzrecv.at[j], zp(j)) for j in range(1, 8)]

    each_halo(kinds[:8], lambda dr, dc, outer: halo_copy(-dr, -dc, outer).wait_recv())
    for cp in t_z:
        cp.start()
    shift_row(1)
    shift_row(TR + 2)
    for i in range(1, TR + 3):
        shift_edges(i)
    first = xs[1, 1 : TR + 3, 0:8].astype(f32)
    last = xs[1, 1 : TR + 3, TC - 8 : TC].astype(f32)
    lcols = left[...].astype(f32)
    rcols = right[...].astype(f32)
    mid_l, mid_r = lcols[1 : TR + 3], rcols[1 : TR + 3]
    sides = ((mid_l[:, 7], first[:, 0], first[:, 1]), (last[:, 6], last[:, 7], mid_r[:, 0]))
    for s, cols in enumerate(sides):
        for b in range(3):
            for a in range(3):
                k = (a * 3 + b) * CI
                edgex[8 * s : 8 * s + 8, k : k + CI] = cols[b][a : a + 8]
    lhs = [
        jnp.concatenate([one, two, edgex[:, k * CI : k * CI + CI].astype(bf16)], axis=0)
        for k, (one, two) in enumerate(zip(taps(0, 1), taps(7, 1), strict=True))
    ]
    feat, slope = gelu_pair(conv(lhs))
    slope = slope * scale
    feats[TC : 2 * TC] = feat[0:TC].astype(bf16)
    deriv[TC : 2 * TC] = slope[0:TC]
    feats[8 * TC : 9 * TC] = feat[TC : 2 * TC].astype(bf16)
    deriv[8 * TC : 9 * TC] = slope[TC : 2 * TC]
    edge_f, edge_d = feat[2 * TC :], slope[2 * TC :]
    corner = jnp.logical_or(sub16 % 8 == 0, sub16 % 8 == 7)
    add_gram(jnp.concatenate([feat[0 : 2 * TC], jnp.where(corner, 0.0, edge_f)], axis=0).astype(bf16), False)

    own_half = pl.multiple_of(core * 768, 768)
    other_half = pl.multiple_of((1 - core) * 768, 768)
    s0[...] = pan[pl.ds(other_half, 768)].astype(bf16)
    g_sib = rcopy(s0, r0, send.at[8], srecv, sib)
    g_sib.start()
    for cp in t_z:
        cp.wait_recv()
    for zz in range(2):
        for b in range(2):
            rows16 = jnp.concatenate([tz[q * 2 + zz][b * 4 : b * 4 + 4] for q in range(4)], axis=0)
            tc[(zz * 2 + b) * 16 : (zz * 2 + b) * 16 + 16] = rows16.astype(bf16)
    g_sib.wait_recv()
    half = pan[pl.ds(own_half, 768)] + r0[...].astype(f32)
    s1[...] = half.astype(bf16)
    pan[pl.ds(own_half, 768)] = half

    g_xy = []
    for j in range(1, 16):
        k = xyk(j)
        g_xy.append(
            rcopy(s1.at[pl.ds(pl.multiple_of(48 * k, 16), 48)], r1.at[j], send.at[8 + j], xrecv.at[j], xyp(j))
        )
    for cp in g_xy:
        cp.start()
    own_t = tb.at[core, pl.ds(pl.multiple_of(64 * xy, 64), 64)]
    t_xy = [rcopy(tc, own_t, send.at[23 + j], txrecv.at[j], xyp(j)) for j in range(1, 16)]
    for cp in t_xy:
        cp.start()
    tb[core, pl.ds(pl.multiple_of(64 * xy, 64), 64)] = tc[...]

    for h in range(1, 7):
        for s, (at, place) in enumerate((((h + 1) * TC, 0), ((h + 2) * TC - 16, 15))):
            put_row(feats, at, place, edge_f[8 * s + h : 8 * s + h + 1])
            put_row(deriv, at, place, edge_d[8 * s + h : 8 * s + h + 1])
    each_halo(kinds[8:], lambda dr, dc, outer: halo_copy(-dr, -dc, outer).wait_recv())
    for i in (0, TR + 3):
        shift_row(i)
        shift_edges(i)
    up_on = jnp.where(has_up, scale, 0.0).astype(f32)
    dn_on = jnp.where(has_dn, scale, 0.0).astype(f32)
    lf_on = jnp.where(has_lf, 1.0, 0.0).astype(f32)
    rt_on = jnp.where(has_rt, 1.0, 0.0).astype(f32)
    ringx[...] = jnp.zeros(ringx.shape, f32)
    first = xs[1, :, 0:8].astype(f32)
    last = xs[1, :, TC - 8 : TC].astype(f32)
    sides = ((lcols[:, 6], lcols[:, 7], first[:, 0]), (last[:, 7], rcols[:, 0], rcols[:, 1]))
    for s, cols in enumerate(sides):
        for b in range(3):
            for a in range(3):
                k = (a * 3 + b) * CI
                ringx[16 * s : 16 * s + 10, k : k + CI] = cols[b][a : a + 10]
    lhs = [
        jnp.concatenate([one, two, ringx[:, k * CI : k * CI + CI].astype(bf16)], axis=0)
        for k, (one, two) in enumerate(zip(taps(-1, 1), taps(8, 1), strict=True))
    ]
    feat, slope = gelu_pair(conv(lhs))
    feats[0:TC] = feat[0:TC].astype(bf16)
    deriv[0:TC] = slope[0:TC] * up_on
    feats[9 * TC : 10 * TC] = feat[TC : 2 * TC].astype(bf16)
    deriv[9 * TC : 10 * TC] = slope[TC : 2 * TC] * dn_on
    ring_row = lax.broadcasted_iota(jnp.int32, (32, CO), 0)
    side_on = jnp.where(ring_row < 16, lf_on, rt_on)
    pos = ring_row % 16
    row_on = jnp.where(pos == 0, up_on, jnp.where(pos == 9, dn_on, jnp.where(pos < 9, scale, 0.0)))
    feats[RING : RING + 32] = feat[2 * TC :].astype(bf16)
    deriv[RING : RING + 32] = slope[2 * TC :] * (side_on * row_on)

    own48 = pl.multiple_of(own_half + 48 * xy, 16)
    acc = pan[pl.ds(own48, 48)]
    for j in range(1, 16):
        g_xy[j - 1].wait_recv()
        acc = acc + r1[j].astype(f32)
    s2[...] = acc.astype(bf16)

    g_z = [rcopy(s2, r2.at[j], send.at[38 + j], zrecv.at[j], zp(j)) for j in range(1, 8)]
    for cp in g_z:
        cp.start()
    for cp in t_xy:
        cp.wait_recv()
    t_fw = rcopy(tb.at[core], tb.at[core], send.at[46], tfrecv, sib)
    t_fw.start()
    for a in range(3):
        for b in range(3):
            wt[a * CO : a * CO + CO, b * CI : b * CI + CI] = wv[3 * a + b].T
    acc = s2[...].astype(f32)
    for j in range(1, 8):
        g_z[j - 1].wait_recv()
        acc = acc + r2[j].astype(f32)
    gf[pl.ds(own48, 48)] = (acc * (1.0 / NPIX)).astype(bf16)

    own_g = gf.at[pl.ds(own48, 48)]
    g_ag = [rcopy(own_g, own_g, send.at[46 + j], arecv.at[j], xyp(j)) for j in range(1, 16)]
    for cp in g_ag:
        cp.start()

    t_fw.wait_recv()

    def tquad(i, k):
        halves = []
        for q in range(2):
            blk = tb[k].reshape(16, 4, 16, 128)[:, i * 2 + q].reshape(256, 128)
            halves.append(blk.astype(f32))
        return jnp.concatenate(halves, axis=1)

    t01 = tquad(0, 1) + tquad(1, 0).T
    t00 = tquad(0, 0)
    t11 = tquad(1, 1)
    tt[0] = t00 + t00.T
    tt[1] = t01
    tt[2] = t01.T
    tt[3] = t11 + t11.T

    g_fw = [rcopy(own_g, own_g, send.at[62], frecv.at[0], sib)]
    g_fw[0].start()
    for j in range(15, 0, -1):
        g_ag[j - 1].wait_recv()
        got = gf.at[pl.ds(pl.multiple_of(own_half + 48 * xyk(j, -1), 16), 48)]
        g_fw.append(rcopy(got, got, send.at[62 + j], frecv.at[j], sib))
        g_fw[-1].start()
    for cp in g_fw:
        cp.wait_recv()

    def gquad(q):
        return jnp.concatenate([gf[q * 512 : q * 512 + 256], gf[q * 512 + 256 : q * 512 + 512]], axis=1).astype(f32)

    g00, g01, g11 = gquad(0), gquad(1), gquad(2)
    g10 = g01.T
    sym[0:256, 0:256] = (2.0 * g00 - tt[0]).astype(bf16)
    sym[0:256, 256:512] = (2.0 * g01 - tt[1]).astype(bf16)
    sym[256:512, 0:256] = (2.0 * g10 - tt[2]).astype(bf16)
    sym[256:512, 256:512] = (2.0 * g11 - tt[3]).astype(bf16)
    gfull[0:256, 0:256] = g00
    gfull[0:256, 256:512] = g01
    gfull[256:512, 0:256] = g10
    gfull[256:512, 256:512] = g11

    for t in range(2):
        at = t * 5 * TC
        up = jnp.dot(feats[at : at + 5 * TC], sym[...], preferred_element_type=f32)
        gp[at : at + 5 * TC] = (up * deriv[at : at + 5 * TC]).astype(bf16)
    upr = jnp.dot(feats[RING : RING + 32], sym[...], preferred_element_type=f32)
    gring[...] = (upr * deriv[RING : RING + 32]).astype(bf16).astype(f32)

    for s, b in ((0, 2), (1, 0)):
        total = jnp.zeros((8, CI), f32)
        for a in range(3):
            rows8 = gring[16 * s + 2 - a : 16 * s + 10 - a].astype(bf16)
            total = total + jnp.dot(
                rows8, wt[a * CO : a * CO + CO, b * CI : b * CI + CI], preferred_element_type=f32
            )
        for h in range(TR):
            edge[s, h] = total[h : h + 1]

    outs = []
    for t in range(2):
        lhs = jnp.concatenate([gp[(4 * t + 2 - a) * TC : (4 * t + 6 - a) * TC] for a in range(3)], axis=1)
        total = jnp.dot(lhs, wt[...], preferred_element_type=f32)
        for i in range(4):
            h = 4 * t + i
            rows = total[i * TC : (i + 1) * TC]
            p0 = jnp.where(lane_row == TC - 1, edge[1, h], pltpu.roll(rows[:, 0:CI], TC - 1, axis=0))
            p2 = jnp.where(lane_row == 0, edge[0, h], pltpu.roll(rows[:, 2 * CI :], 1, axis=0))
            outv[h] = (rows[:, CI : 2 * CI] + p0 + p2).astype(bf16)
        outs.append(pltpu.make_async_copy(outv.at[pl.ds(4 * t, 4)], grad_out.at[pl.ds(4 * t, 4)], osem.at[t]))
        outs[t].start()

    own_row = zl * 256 + xy * 16 + zh * 4 + core * 2
    rows8 = gfull[pl.ds(pl.multiple_of((own_row // 8) * 8, 8), 8)]
    sub = lax.broadcasted_iota(jnp.int32, (8, CO), 0)
    for k in range(2):
        outg[k : k + 1] = jnp.sum(jnp.where(sub == own_row % 8 + k, rows8, 0.0), axis=0, keepdims=True)
    g_out = pltpu.make_async_copy(outg, gram_out, osem.at[4])
    g_out.start()
    g_out.wait()
    for cp in outs:
        cp.wait()
    each_halo(kinds, lambda dr, dc, outer: halo_copy(dr, dc, outer).wait_send())
    for cp in [t_sib, g_sib, t_fw] + g_fw + t_z + g_xy + t_xy + g_z + g_ag:
        cp.wait_send()


def finish(gram, grad, gram_out, grad_out, sem):
    one = pltpu.make_async_copy(gram, gram_out, sem.at[0])
    two = pltpu.make_async_copy(grad, grad_out, sem.at[1])
    one.start()
    two.start()
    one.wait()
    two.wait()


def on_device(canvas, conv_weight, conv_bias, target_gram):
    hbm = pl.BlockSpec(memory_space=pl.ANY)
    vmem = pl.BlockSpec(memory_space=pltpu.VMEM)
    dma = pltpu.SemaphoreType.DMA
    shapes = (jax.ShapeDtypeStruct((2, CO), f32), jax.ShapeDtypeStruct((TR, TC, CI), bf16))
    gram, grad = pl.pallas_call(
        kernel,
        out_shape=shapes,
        in_specs=[hbm, hbm, vmem, hbm],
        out_specs=(hbm, hbm),
        scratch_shapes=[
            pltpu.VMEM((3, TR + 4, TC, CI), bf16),
            pltpu.VMEM((TR + 4, 8, CI), bf16),
            pltpu.VMEM((TR + 4, 8, CI), bf16),
            pltpu.VMEM((9, CI, CO), bf16),
            pltpu.VMEM((3 * CO, 3 * CI), bf16),
            pltpu.VMEM((RING + 32, CO), bf16),
            pltpu.VMEM((RING + 32, CO), f32),
            pltpu.VMEM((RING, CO), bf16),
            pltpu.VMEM((32, CO), f32),
            pltpu.VMEM((32, 9 * CI), f32),
            pltpu.VMEM((16, 9 * CI), f32),
            pltpu.VMEM((1536, 128), f32),
            pltpu.VMEM((768, 128), bf16),
            pltpu.VMEM((768, 128), bf16),
            pltpu.VMEM((768, 128), bf16),
            pltpu.VMEM((16, 48, 128), bf16),
            pltpu.VMEM((48, 128), bf16),
            pltpu.VMEM((8, 48, 128), bf16),
            pltpu.VMEM((1536, 128), bf16),
            pltpu.VMEM((CO, CO), bf16),
            pltpu.VMEM((4, 256, 256), f32),
            pltpu.VMEM((CO, CO), f32),
            pltpu.VMEM((2, 2, CO), f32),
            pltpu.VMEM((8, 8, 128), f32),
            pltpu.VMEM((64, 128), bf16),
            pltpu.VMEM((2, 1024, 128), bf16),
            pltpu.VMEM((TR, TC, CI), bf16),
            pltpu.VMEM((2, CO), f32),
            pltpu.VMEM((2, TR, 1, CI), f32),
            dma((3,)),
            dma((10,)),
            dma((10,)),
            dma((78,)),
            dma((16,)),
            dma((8,)),
            dma((16,)),
            dma((16,)),
            dma,
            dma,
            dma((8,)),
            dma((16,)),
            dma,
            dma((5,)),
        ],
        compiler_params=pltpu.CompilerParams(
            collective_id=0, has_side_effects=True, vmem_limit_bytes=56 * 1024 * 1024
        ),
        name="style_grad",
    )(canvas, conv_weight.reshape(9, CI, CO), conv_bias, target_gram)
    return pl.pallas_call(
        finish, out_shape=shapes, in_specs=[hbm, hbm], out_specs=(hbm, hbm), scratch_shapes=[dma((2,))], name="finish"
    )(gram, grad)


def solution(mesh):
    return jax.shard_map(
        on_device,
        mesh=mesh,
        in_specs=(P("rows", "cols", None), P(), P(), P(("rows", "cols"), None)),
        out_specs=(P(("rows", "cols"), None), P("rows", "cols", None)),
        check_vma=False,
    )
```

```python
import math

import jax
import jax.numpy as jnp
from jax import lax
from jax.experimental import pallas as pl
from jax.experimental.pallas import tpu as pltpu
from jax.sharding import PartitionSpec as P

MESH = pl.DeviceIdType.MESH
f32, bf16 = jnp.float32, jnp.bfloat16
C0 = math.sqrt(2.0 / math.pi)
C1 = C0 * 0.044715
TR, TC, CI, CO = 8, 128, 256, 512
NPIX = 262144
NR, NC = 32, 8
RING = 10 * TC
XY_STEPS = sorted(
    ((i, j) for i in range(4) for j in range(4) if i or j), key=lambda s: (-min(s[0], 4 - s[0]) - min(s[1], 4 - s[1]), s)
)
Z_STEPS = (4, 3, 5, 2, 6, 1, 7)


def gelu_pair(v):
    square = v * v
    half = 0.5 + 0.5 * jnp.tanh(v * (C0 + C1 * square))
    feat = v * half
    slope = half + feat * (1.0 - half) * (2.0 * C0 + 6.0 * C1 * square)
    return feat, slope


def kernel(
    canvas, weight, bias, target, outg, outv,
    xs, left, right, wv, wt, feats, deriv, gp, gring, ringx, edgex, pan, s0, r0, s1, r1, s2, r2, gf,
    sym, tt, gfull, t2, tz, tc, tb, edge,
    lsem, hsend, hrecv, send, xrecv, zrecv, arecv, frecv, srecv, tsrecv, tzrecv, txrecv, tfrecv,
):
    r = lax.axis_index("rows")
    c = lax.axis_index("cols")
    xy, zl, core, zh = r % 16, r // 16, c % 2, c // 2
    z = zh * 2 + zl
    sib = (r, c + 1 - 2 * core)

    x, y = xy % 4, xy // 4

    def xyk(j, sign=1):
        dx, dy = XY_STEPS[j - 1]
        return (x + sign * dx + 4) % 4 + 4 * ((y + sign * dy + 4) % 4)

    def xyp(j):
        return (zl * 16 + xyk(j), c)

    def zp(j):
        z2 = (z + Z_STEPS[j - 1]) % 8
        return ((z2 % 2) * 16 + xy, (z2 // 2) * 2 + core)

    def rcopy(src, dst, ssem, rsem, dev):
        return pltpu.make_async_remote_copy(
            src_ref=src, dst_ref=dst, send_sem=ssem, recv_sem=rsem, device_id=dev, device_id_type=MESH
        )

    ld_canvas = pltpu.make_async_copy(canvas, xs.at[1, pl.ds(2, TR)], lsem.at[0])
    ld_weight = pltpu.make_async_copy(weight, wv, lsem.at[1])
    ld_target = pltpu.make_async_copy(target, t2.at[core], lsem.at[2])
    ld_canvas.start()
    ld_weight.start()
    ld_target.start()

    has_up, has_dn, has_lf, has_rt = r > 0, r < NR - 1, c > 0, c < NC - 1
    halo = []
    for dr in (-1, 0, 1):
        for dc in (-1, 0, 1):
            if dr == 0 and dc == 0:
                continue
            cond = None
            for step, flag in ((dr, (has_up, has_dn)), (dc, (has_lf, has_rt))):
                if step:
                    this = flag[0] if step < 0 else flag[1]
                    cond = this if cond is None else jnp.logical_and(cond, this)
            halo.append((dr, dc, cond))
    bar = pltpu.get_barrier_semaphore()
    count = jnp.int32(23)
    for dr, dc, cond in halo:
        count = count + jnp.where(cond, 1, 0)

        @pl.when(cond)
        def _():
            pl.semaphore_signal(bar, inc=1, device_id=(r + dr, c + dc), device_id_type=MESH)

    pl.semaphore_signal(bar, inc=1, device_id=sib, device_id_type=MESH)
    for j in range(1, 16):
        pl.semaphore_signal(bar, inc=1, device_id=xyp(j), device_id_type=MESH)
    for j in range(1, 8):
        pl.semaphore_signal(bar, inc=1, device_id=zp(j), device_id_type=MESH)
    pl.semaphore_wait(bar, count)

    kinds = [(dr, dc, 0) for dr, dc, _ in halo]
    kinds = [(-1, 0, 0), (1, 0, 0)] + [k for k in kinds if k[1]] + [(-1, 0, 1), (1, 0, 1)]
    flags = {(dr, dc): cond for dr, dc, cond in halo}

    def halo_copy(dr, dc, outer):
        k = kinds.index((dr, dc, outer))
        if dc == 0:
            src = canvas.at[outer] if dr < 0 else canvas.at[TR - 1 - outer]
            dst = xs.at[1, TR + 2 + outer] if dr < 0 else xs.at[1, 1 - outer]
        else:
            rows_src = pl.ds(0, 2) if dr < 0 else (pl.ds(TR - 2, 2) if dr > 0 else pl.ds(0, TR))
            rows_dst = pl.ds(TR + 2, 2) if dr < 0 else (pl.ds(0, 2) if dr > 0 else pl.ds(2, TR))
            if dc < 0:
                src, dst = canvas.at[rows_src, pl.ds(0, 8)], right.at[rows_dst]
            else:
                src, dst = canvas.at[rows_src, pl.ds(TC - 8, 8)], left.at[rows_dst]
        return rcopy(src, dst, hsend.at[k], hrecv.at[k], (r + dr, c + dc))

    def each_halo(some, act):
        for dr, dc, outer in some:

            @pl.when(flags[dr, dc])
            def _():
                act(dr, dc, outer)

    each_halo(kinds, lambda dr, dc, outer: halo_copy(dr, dc, outer).start())

    t_sib = rcopy(target, t2.at[core], send.at[0], tsrecv, sib)
    t_sib.start()

    @pl.when(r == 0)
    def _():
        xs[1, 0:2] = jnp.zeros((2, TC, CI), bf16)
        left[0:2] = jnp.zeros((2, 8, CI), bf16)
        right[0:2] = jnp.zeros((2, 8, CI), bf16)

    @pl.when(r == NR - 1)
    def _():
        xs[1, TR + 2 : TR + 4] = jnp.zeros((2, TC, CI), bf16)
        left[TR + 2 : TR + 4] = jnp.zeros((2, 8, CI), bf16)
        right[TR + 2 : TR + 4] = jnp.zeros((2, 8, CI), bf16)

    @pl.when(c == 0)
    def _():
        left[...] = jnp.zeros((TR + 4, 8, CI), bf16)

    @pl.when(c == NC - 1)
    def _():
        right[...] = jnp.zeros((TR + 4, 8, CI), bf16)

    lane_row = lax.broadcasted_iota(jnp.int32, (TC, CI), 0)

    def shift_row(i):
        row = xs[1, i].astype(f32)
        xs[0, i] = pltpu.roll(row, 1, axis=0).astype(bf16)
        xs[2, i] = pltpu.roll(row, TC - 1, axis=0).astype(bf16)

    def shift_edges(i):
        sub = lax.broadcasted_iota(jnp.int32, (16, CI), 0)
        top = xs[0, i, 0:16].astype(f32)
        xs[0, i, 0:16] = jnp.where(sub == 0, left[i].astype(f32)[7:8], top).astype(bf16)
        bot = xs[2, i, TC - 16 : TC].astype(f32)
        xs[2, i, TC - 16 : TC] = jnp.where(sub == 15, right[i].astype(f32)[0:1], bot).astype(bf16)

    ld_canvas.wait()

    def shift_own(i, carry):
        shift_row(i + 2)
        return carry

    lax.fori_loop(0, TR, shift_own, 0)
    ld_target.wait()
    t_sib.wait_recv()
    quads = []
    for b in range(2):
        for q in range(2):
            rows2 = t2[q]
            quads.append(
                jnp.where(core == 0, rows2[:, b * 128 : b * 128 + 128], rows2[:, 256 + b * 128 : 384 + b * 128])
            )
    tz[z] = jnp.concatenate(quads, axis=0)
    t_z = [rcopy(tz.at[z], tz.at[z], send.at[j], tzrecv.at[j], zp(j)) for j in range(1, 8)]
    for cp in t_z:
        cp.start()

    ld_weight.wait()
    bias_row = bias[...].astype(f32).reshape(1, CO)
    wflat = wv.reshape(9 * CI, CO)

    def conv(parts):
        lhs = jnp.concatenate(parts, axis=1)
        return jnp.dot(lhs, wflat[...], preferred_element_type=f32) + bias_row

    def taps(h, n):
        return [xs[b, h + a + 1 : h + a + 1 + n].reshape(n * TC, CI) for a in range(3) for b in range(3)]

    scale = 1.0 / math.sqrt(CO)

    def add_gram(feat, fresh):
        lo, hi = feat[:, 0:256], feat[:, 256:512]
        for q, (one, two) in enumerate(((lo, lo), (lo, hi), (hi, hi))):
            prod = lax.dot_general(one, two, (((0,), (0,)), ((), ())), preferred_element_type=f32)
            for s in range(2):
                at = (2 * q + s) * 256
                part = prod[:, s * 128 : s * 128 + 128]
                pan[at : at + 256] = part if fresh else pan[at : at + 256] + part

    feat, slope = gelu_pair(conv(taps(1, 6)))
    feats[2 * TC : 8 * TC] = feat.astype(bf16)
    deriv[2 * TC : 8 * TC] = slope * scale
    sub16 = lax.broadcasted_iota(jnp.int32, (16, CO), 0)

    def put_row(ref, at, place, row):
        old = ref[at : at + 16].astype(f32)
        ref[at : at + 16] = jnp.where(sub16 == place, row, old).astype(ref.dtype)

    for h in range(1, 7):
        put_row(feats, (h + 1) * TC, 0, 0.0)
        put_row(feats, (h + 2) * TC - 16, 15, 0.0)
    add_gram(feats[2 * TC : 8 * TC], True)

    each_halo(kinds[:8], lambda dr, dc, outer: halo_copy(-dr, -dc, outer).wait_recv())
    shift_row(1)
    shift_row(TR + 2)
    for i in range(1, TR + 3):
        shift_edges(i)
    first = xs[1, 1 : TR + 3, 0:8].astype(f32)
    last = xs[1, 1 : TR + 3, TC - 8 : TC].astype(f32)
    lcols = left[...].astype(f32)
    rcols = right[...].astype(f32)
    mid_l, mid_r = lcols[1 : TR + 3], rcols[1 : TR + 3]
    sides = ((mid_l[:, 7], first[:, 0], first[:, 1]), (last[:, 6], last[:, 7], mid_r[:, 0]))
    for s, cols in enumerate(sides):
        for b in range(3):
            for a in range(3):
                k = (a * 3 + b) * CI
                edgex[8 * s : 8 * s + 8, k : k + CI] = cols[b][a : a + 8]
    lhs = [
        jnp.concatenate([one, two, edgex[:, k * CI : k * CI + CI].astype(bf16)], axis=0)
        for k, (one, two) in enumerate(zip(taps(0, 1), taps(7, 1), strict=True))
    ]
    feat, slope = gelu_pair(conv(lhs))
    slope = slope * scale
    feats[TC : 2 * TC] = feat[0:TC].astype(bf16)
    deriv[TC : 2 * TC] = slope[0:TC]
    feats[8 * TC : 9 * TC] = feat[TC : 2 * TC].astype(bf16)
    deriv[8 * TC : 9 * TC] = slope[TC : 2 * TC]
    edge_f, edge_d = feat[2 * TC :], slope[2 * TC :]
    corner = jnp.logical_or(sub16 % 8 == 0, sub16 % 8 == 7)
    add_gram(jnp.concatenate([feat[0 : 2 * TC], jnp.where(corner, 0.0, edge_f)], axis=0).astype(bf16), False)

    own_half = pl.multiple_of(core * 768, 768)
    other_half = pl.multiple_of((1 - core) * 768, 768)
    s0[...] = pan[pl.ds(other_half, 768)].astype(bf16)
    g_sib = rcopy(s0, r0, send.at[8], srecv, sib)
    g_sib.start()
    g_sib.wait_recv()
    half = pan[pl.ds(own_half, 768)] + r0[...].astype(f32)
    s1[...] = half.astype(bf16)
    pan[pl.ds(own_half, 768)] = half

    g_xy = []
    for j in range(1, 16):
        k = xyk(j)
        g_xy.append(
            rcopy(s1.at[pl.ds(pl.multiple_of(48 * k, 16), 48)], r1.at[j], send.at[8 + j], xrecv.at[j], xyp(j))
        )
    for cp in g_xy:
        cp.start()
    for h in range(1, 7):
        for s, (at, place) in enumerate((((h + 1) * TC, 0), ((h + 2) * TC - 16, 15))):
            put_row(feats, at, place, edge_f[8 * s + h : 8 * s + h + 1])
            put_row(deriv, at, place, edge_d[8 * s + h : 8 * s + h + 1])
    each_halo(kinds[8:], lambda dr, dc, outer: halo_copy(-dr, -dc, outer).wait_recv())
    for i in (0, TR + 3):
        shift_row(i)
        shift_edges(i)
    up_on = jnp.where(has_up, scale, 0.0).astype(f32)
    dn_on = jnp.where(has_dn, scale, 0.0).astype(f32)
    lf_on = jnp.where(has_lf, 1.0, 0.0).astype(f32)
    rt_on = jnp.where(has_rt, 1.0, 0.0).astype(f32)
    ringx[...] = jnp.zeros(ringx.shape, f32)
    first = xs[1, :, 0:8].astype(f32)
    last = xs[1, :, TC - 8 : TC].astype(f32)
    sides = ((lcols[:, 6], lcols[:, 7], first[:, 0]), (last[:, 7], rcols[:, 0], rcols[:, 1]))
    for s, cols in enumerate(sides):
        for b in range(3):
            for a in range(3):
                k = (a * 3 + b) * CI
                ringx[16 * s : 16 * s + 10, k : k + CI] = cols[b][a : a + 10]
    lhs = [
        jnp.concatenate([one, two, ringx[:, k * CI : k * CI + CI].astype(bf16)], axis=0)
        for k, (one, two) in enumerate(zip(taps(-1, 1), taps(8, 1), strict=True))
    ]
    feat, slope = gelu_pair(conv(lhs))
    feats[0:TC] = feat[0:TC].astype(bf16)
    deriv[0:TC] = slope[0:TC] * up_on
    feats[9 * TC : 10 * TC] = feat[TC : 2 * TC].astype(bf16)
    deriv[9 * TC : 10 * TC] = slope[TC : 2 * TC] * dn_on
    ring_row = lax.broadcasted_iota(jnp.int32, (32, CO), 0)
    side_on = jnp.where(ring_row < 16, lf_on, rt_on)
    pos = ring_row % 16
    row_on = jnp.where(pos == 0, up_on, jnp.where(pos == 9, dn_on, jnp.where(pos < 9, scale, 0.0)))
    feats[RING : RING + 32] = feat[2 * TC :].astype(bf16)
    deriv[RING : RING + 32] = slope[2 * TC :] * (side_on * row_on)

    for cp in t_z:
        cp.wait_recv()
    for zz in range(2):
        for b in range(2):
            rows16 = jnp.concatenate([tz[q * 2 + zz][b * 4 : b * 4 + 4] for q in range(4)], axis=0)
            tc[(zz * 2 + b) * 16 : (zz * 2 + b) * 16 + 16] = rows16.astype(bf16)
    own_t = tb.at[core, pl.ds(pl.multiple_of(64 * xy, 64), 64)]
    t_xy = [rcopy(tc, own_t, send.at[23 + j], txrecv.at[j], xyp(j)) for j in range(1, 16)]
    for cp in t_xy:
        cp.start()
    tb[core, pl.ds(pl.multiple_of(64 * xy, 64), 64)] = tc[...]

    own48 = pl.multiple_of(own_half + 48 * xy, 16)
    acc = pan[pl.ds(own48, 48)]
    for j in range(1, 16):
        g_xy[j - 1].wait_recv()
        acc = acc + r1[j].astype(f32)
    s2[...] = acc.astype(bf16)

    g_z = [rcopy(s2, r2.at[j], send.at[38 + j], zrecv.at[j], zp(j)) for j in range(1, 8)]
    for cp in g_z:
        cp.start()
    for a in range(3):
        for b in range(3):
            wt[a * CO : a * CO + CO, b * CI : b * CI + CI] = wv[3 * a + b].T
    acc = s2[...].astype(f32)
    for j in range(1, 8):
        g_z[j - 1].wait_recv()
        acc = acc + r2[j].astype(f32)
    gf[pl.ds(own48, 48)] = (acc * (1.0 / NPIX)).astype(bf16)

    own_g = gf.at[pl.ds(own48, 48)]
    g_ag = [rcopy(own_g, own_g, send.at[46 + j], arecv.at[j], xyp(j)) for j in range(1, 16)]
    for cp in g_ag:
        cp.start()

    for cp in t_xy:
        cp.wait_recv()
    t_fw = rcopy(tb.at[core], tb.at[core], send.at[46], tfrecv, sib)
    t_fw.start()
    t_fw.wait_recv()

    def tquad(i, k):
        halves = []
        for q in range(2):
            blk = tb[k].reshape(16, 4, 16, 128)[:, i * 2 + q].reshape(256, 128)
            halves.append(blk.astype(f32))
        return jnp.concatenate(halves, axis=1)

    t01 = tquad(0, 1) + tquad(1, 0).T
    t00 = tquad(0, 0)
    t11 = tquad(1, 1)
    tt[0] = t00 + t00.T
    tt[1] = t01
    tt[2] = t01.T
    tt[3] = t11 + t11.T

    g_fw = [rcopy(own_g, own_g, send.at[62], frecv.at[0], sib)]
    g_fw[0].start()
    for j in range(15, 0, -1):
        g_ag[j - 1].wait_recv()
        got = gf.at[pl.ds(pl.multiple_of(own_half + 48 * xyk(j, -1), 16), 48)]
        g_fw.append(rcopy(got, got, send.at[62 + j], frecv.at[j], sib))
        g_fw[-1].start()
    for cp in g_fw:
        cp.wait_recv()

    def gquad(q):
        return jnp.concatenate([gf[q * 512 : q * 512 + 256], gf[q * 512 + 256 : q * 512 + 512]], axis=1).astype(f32)

    g00, g01, g11 = gquad(0), gquad(1), gquad(2)
    g10 = g01.T
    sym[0:256, 0:256] = (2.0 * g00 - tt[0]).astype(bf16)
    sym[0:256, 256:512] = (2.0 * g01 - tt[1]).astype(bf16)
    sym[256:512, 0:256] = (2.0 * g10 - tt[2]).astype(bf16)
    sym[256:512, 256:512] = (2.0 * g11 - tt[3]).astype(bf16)
    gfull[0:256, 0:256] = g00
    gfull[0:256, 256:512] = g01
    gfull[256:512, 0:256] = g10
    gfull[256:512, 256:512] = g11

    for t in range(2):
        at = t * 5 * TC
        up = jnp.dot(feats[at : at + 5 * TC], sym[...], preferred_element_type=f32)
        gp[at : at + 5 * TC] = (up * deriv[at : at + 5 * TC]).astype(bf16)
    upr = jnp.dot(feats[RING : RING + 32], sym[...], preferred_element_type=f32)
    gring[...] = (upr * deriv[RING : RING + 32]).astype(bf16).astype(f32)

    for s, b in ((0, 2), (1, 0)):
        total = jnp.zeros((8, CI), f32)
        for a in range(3):
            rows8 = gring[16 * s + 2 - a : 16 * s + 10 - a].astype(bf16)
            total = total + jnp.dot(
                rows8, wt[a * CO : a * CO + CO, b * CI : b * CI + CI], preferred_element_type=f32
            )
        for h in range(TR):
            edge[s, h] = total[h : h + 1]

    for t in range(2):
        lhs = jnp.concatenate([gp[(4 * t + 2 - a) * TC : (4 * t + 6 - a) * TC] for a in range(3)], axis=1)
        total = jnp.dot(lhs, wt[...], preferred_element_type=f32)
        for i in range(4):
            h = 4 * t + i
            rows = total[i * TC : (i + 1) * TC]
            p0 = jnp.where(lane_row == TC - 1, edge[1, h], pltpu.roll(rows[:, 0:CI], TC - 1, axis=0))
            p2 = jnp.where(lane_row == 0, edge[0, h], pltpu.roll(rows[:, 2 * CI :], 1, axis=0))
            outv[h] = (rows[:, CI : 2 * CI] + p0 + p2).astype(bf16)

    own_row = zl * 256 + xy * 16 + zh * 4 + core * 2
    rows8 = gfull[pl.ds(pl.multiple_of((own_row // 8) * 8, 8), 8)]
    sub = lax.broadcasted_iota(jnp.int32, (8, CO), 0)
    for k in range(2):
        outg[k : k + 1] = jnp.sum(jnp.where(sub == own_row % 8 + k, rows8, 0.0), axis=0, keepdims=True)
    each_halo(kinds, lambda dr, dc, outer: halo_copy(dr, dc, outer).wait_send())
    for cp in [t_sib, g_sib, t_fw] + g_fw + t_z + g_xy + t_xy + g_z + g_ag:
        cp.wait_send()


def finish(gram, grad, gram_out, grad_out, sem):
    one = pltpu.make_async_copy(gram, gram_out, sem.at[0])
    two = pltpu.make_async_copy(grad, grad_out, sem.at[1])
    two.start()
    one.start()
    one.wait()
    two.wait()


def on_device(canvas, conv_weight, conv_bias, target_gram):
    hbm = pl.BlockSpec(memory_space=pl.ANY)
    vmem = pl.BlockSpec(memory_space=pltpu.VMEM)
    dma = pltpu.SemaphoreType.DMA
    held = (pltpu.VMEM((2, CO), f32), pltpu.VMEM((TR, TC, CI), bf16))
    shapes = (jax.ShapeDtypeStruct((2, CO), f32), jax.ShapeDtypeStruct((TR, TC, CI), bf16))
    gram, grad = pl.pallas_call(
        kernel,
        out_shape=held,
        in_specs=[hbm, hbm, vmem, hbm],
        out_specs=(vmem, vmem),
        scratch_shapes=[
            pltpu.VMEM((3, TR + 4, TC, CI), bf16),
            pltpu.VMEM((TR + 4, 8, CI), bf16),
            pltpu.VMEM((TR + 4, 8, CI), bf16),
            pltpu.VMEM((9, CI, CO), bf16),
            pltpu.VMEM((3 * CO, 3 * CI), bf16),
            pltpu.VMEM((RING + 32, CO), bf16),
            pltpu.VMEM((RING + 32, CO), f32),
            pltpu.VMEM((RING, CO), bf16),
            pltpu.VMEM((32, CO), f32),
            pltpu.VMEM((32, 9 * CI), f32),
            pltpu.VMEM((16, 9 * CI), f32),
            pltpu.VMEM((1536, 128), f32),
            pltpu.VMEM((768, 128), bf16),
            pltpu.VMEM((768, 128), bf16),
            pltpu.VMEM((768, 128), bf16),
            pltpu.VMEM((16, 48, 128), bf16),
            pltpu.VMEM((48, 128), bf16),
            pltpu.VMEM((8, 48, 128), bf16),
            pltpu.VMEM((1536, 128), bf16),
            pltpu.VMEM((CO, CO), bf16),
            pltpu.VMEM((4, 256, 256), f32),
            pltpu.VMEM((CO, CO), f32),
            pltpu.VMEM((2, 2, CO), f32),
            pltpu.VMEM((8, 8, 128), f32),
            pltpu.VMEM((64, 128), bf16),
            pltpu.VMEM((2, 1024, 128), bf16),
            pltpu.VMEM((2, TR, 1, CI), f32),
            dma((3,)),
            dma((10,)),
            dma((10,)),
            dma((78,)),
            dma((16,)),
            dma((8,)),
            dma((16,)),
            dma((16,)),
            dma,
            dma,
            dma((8,)),
            dma((16,)),
            dma,
        ],
        compiler_params=pltpu.CompilerParams(
            collective_id=0, has_side_effects=True, vmem_limit_bytes=56 * 1024 * 1024
        ),
        name="style_grad",
    )(canvas, conv_weight.reshape(9, CI, CO), conv_bias, target_gram)
    gram = pltpu.with_memory_space_constraint(gram, pltpu.VMEM)
    grad = pltpu.with_memory_space_constraint(grad, pltpu.VMEM)
    return pl.pallas_call(
        finish, out_shape=shapes, in_specs=[vmem, vmem], out_specs=(hbm, hbm), scratch_shapes=[dma((2,))], name="finish"
    )(gram, grad)


def solution(mesh):
    return jax.shard_map(
        on_device,
        mesh=mesh,
        in_specs=(P("rows", "cols", None), P(), P(), P(("rows", "cols"), None)),
        out_specs=(P(("rows", "cols"), None), P("rows", "cols", None)),
        check_vma=False,
    )
```

```python
import math

import jax
import jax.numpy as jnp
from jax import lax
from jax.experimental import pallas as pl
from jax.experimental.pallas import tpu as pltpu
from jax.sharding import PartitionSpec as P

MESH = pl.DeviceIdType.MESH
f32, bf16 = jnp.float32, jnp.bfloat16
C0 = math.sqrt(2.0 / math.pi)
C1 = C0 * 0.044715
TR, TC, CI, CO = 8, 128, 256, 512
NPIX = 262144
NR, NC = 32, 8
RING = 10 * TC
XY_STEPS = sorted(
    ((i, j) for i in range(4) for j in range(4) if i or j), key=lambda s: (-min(s[0], 4 - s[0]) - min(s[1], 4 - s[1]), s)
)
Z_STEPS = (4, 3, 5, 2, 6, 1, 7)


PANELS = ((0, 0, 128, 0), (0, 1, 256, 128), (1, 0, 256, 384), (1, 1, 256, 640), (2, 0, 128, 896), (2, 1, 256, 1024))
GROWS = 1280
HALF = GROWS // 2
CHUNK = HALF // 16


def gelu_pair(v):
    square = v * v
    half = 0.5 + 0.5 * jnp.tanh(v * (C0 + C1 * square))
    feat = v * half
    slope = half + feat * (1.0 - half) * (2.0 * C0 + 6.0 * C1 * square)
    return feat, slope


def kernel(
    canvas, weight, bias, target, outg, outv,
    xs, left, right, wv, wt, feats, deriv, gp, gring, ringx, edgex, pan, s0, r0, s1, r1, s2, r2, s3, gf,
    sym, tt, gfull, t2, tz, tc, tb, edge,
    lsem, hsend, hrecv, send, xrecv, zrecv, arecv, srecv, tsrecv, tzrecv, txrecv, tfrecv,
):
    r = lax.axis_index("rows")
    c = lax.axis_index("cols")
    xy, zl, core, zh = r % 16, r // 16, c % 2, c // 2
    z = zh * 2 + zl
    sib = (r, c + 1 - 2 * core)

    x, y = xy % 4, xy // 4

    def xyk(j, sign=1):
        dx, dy = XY_STEPS[j - 1]
        return (x + sign * dx + 4) % 4 + 4 * ((y + sign * dy + 4) % 4)

    def xyp(j):
        return (zl * 16 + xyk(j), c)

    def zp(j):
        z2 = (z + Z_STEPS[j - 1]) % 8
        return ((z2 % 2) * 16 + xy, (z2 // 2) * 2 + core)

    def rcopy(src, dst, ssem, rsem, dev):
        return pltpu.make_async_remote_copy(
            src_ref=src, dst_ref=dst, send_sem=ssem, recv_sem=rsem, device_id=dev, device_id_type=MESH
        )

    ld_canvas = pltpu.make_async_copy(canvas, xs.at[1, pl.ds(2, TR)], lsem.at[0])
    ld_weight = pltpu.make_async_copy(weight, wv, lsem.at[1])
    ld_target = pltpu.make_async_copy(target, t2.at[core], lsem.at[2])
    ld_canvas.start()
    ld_weight.start()
    ld_target.start()

    has_up, has_dn, has_lf, has_rt = r > 0, r < NR - 1, c > 0, c < NC - 1
    halo = []
    for dr in (-1, 0, 1):
        for dc in (-1, 0, 1):
            if dr == 0 and dc == 0:
                continue
            cond = None
            for step, flag in ((dr, (has_up, has_dn)), (dc, (has_lf, has_rt))):
                if step:
                    this = flag[0] if step < 0 else flag[1]
                    cond = this if cond is None else jnp.logical_and(cond, this)
            halo.append((dr, dc, cond))
    bar = pltpu.get_barrier_semaphore()
    count = jnp.int32(38)
    for dr, dc, cond in halo:
        count = count + jnp.where(cond, 1, 0)

        @pl.when(cond)
        def _():
            pl.semaphore_signal(bar, inc=1, device_id=(r + dr, c + dc), device_id_type=MESH)

    pl.semaphore_signal(bar, inc=1, device_id=sib, device_id_type=MESH)
    for j in range(1, 16):
        pl.semaphore_signal(bar, inc=1, device_id=xyp(j), device_id_type=MESH)
    for j in range(1, 8):
        pl.semaphore_signal(bar, inc=1, device_id=zp(j), device_id_type=MESH)

    for j in range(1, 16):
        pl.semaphore_signal(bar, inc=1, device_id=(zl * 16 + xyk(j), c + 1 - 2 * core), device_id_type=MESH)

    pl.semaphore_wait(bar, count)

    kinds = [(dr, dc, 0) for dr, dc, _ in halo]
    kinds = [(-1, 0, 0), (1, 0, 0)] + [k for k in kinds if k[1]] + [(-1, 0, 1), (1, 0, 1)]
    flags = {(dr, dc): cond for dr, dc, cond in halo}

    def halo_copy(dr, dc, outer):
        k = kinds.index((dr, dc, outer))
        if dc == 0:
            src = canvas.at[outer] if dr < 0 else canvas.at[TR - 1 - outer]
            dst = xs.at[1, TR + 2 + outer] if dr < 0 else xs.at[1, 1 - outer]
        else:
            rows_src = pl.ds(0, 2) if dr < 0 else (pl.ds(TR - 2, 2) if dr > 0 else pl.ds(0, TR))
            rows_dst = pl.ds(TR + 2, 2) if dr < 0 else (pl.ds(0, 2) if dr > 0 else pl.ds(2, TR))
            if dc < 0:
                src, dst = canvas.at[rows_src, pl.ds(0, 8)], right.at[rows_dst]
            else:
                src, dst = canvas.at[rows_src, pl.ds(TC - 8, 8)], left.at[rows_dst]
        return rcopy(src, dst, hsend.at[k], hrecv.at[k], (r + dr, c + dc))

    def each_halo(some, act):
        for dr, dc, outer in some:

            @pl.when(flags[dr, dc])
            def _():
                act(dr, dc, outer)

    each_halo(kinds, lambda dr, dc, outer: halo_copy(dr, dc, outer).start())

    t_sib = rcopy(target, t2.at[core], send.at[0], tsrecv, sib)
    t_sib.start()

    @pl.when(r == 0)
    def _():
        xs[1, 0:2] = jnp.zeros((2, TC, CI), bf16)
        left[0:2] = jnp.zeros((2, 8, CI), bf16)
        right[0:2] = jnp.zeros((2, 8, CI), bf16)

    @pl.when(r == NR - 1)
    def _():
        xs[1, TR + 2 : TR + 4] = jnp.zeros((2, TC, CI), bf16)
        left[TR + 2 : TR + 4] = jnp.zeros((2, 8, CI), bf16)
        right[TR + 2 : TR + 4] = jnp.zeros((2, 8, CI), bf16)

    @pl.when(c == 0)
    def _():
        left[...] = jnp.zeros((TR + 4, 8, CI), bf16)

    @pl.when(c == NC - 1)
    def _():
        right[...] = jnp.zeros((TR + 4, 8, CI), bf16)

    lane_row = lax.broadcasted_iota(jnp.int32, (TC, CI), 0)

    def shift_row(i):
        row = xs[1, i].astype(f32)
        xs[0, i] = pltpu.roll(row, 1, axis=0).astype(bf16)
        xs[2, i] = pltpu.roll(row, TC - 1, axis=0).astype(bf16)

    def shift_edges(i):
        sub = lax.broadcasted_iota(jnp.int32, (16, CI), 0)
        top = xs[0, i, 0:16].astype(f32)
        xs[0, i, 0:16] = jnp.where(sub == 0, left[i].astype(f32)[7:8], top).astype(bf16)
        bot = xs[2, i, TC - 16 : TC].astype(f32)
        xs[2, i, TC - 16 : TC] = jnp.where(sub == 15, right[i].astype(f32)[0:1], bot).astype(bf16)

    ld_canvas.wait()

    def shift_own(i, carry):
        shift_row(i + 2)
        return carry

    lax.fori_loop(0, TR, shift_own, 0)
    ld_target.wait()
    t_sib.wait_recv()
    quads = []
    for b in range(2):
        for q in range(2):
            rows2 = t2[q]
            quads.append(
                jnp.where(core == 0, rows2[:, b * 128 : b * 128 + 128], rows2[:, 256 + b * 128 : 384 + b * 128])
            )
    tz[z] = jnp.concatenate(quads, axis=0)
    t_z = [rcopy(tz.at[z], tz.at[z], send.at[j], tzrecv.at[j], zp(j)) for j in range(1, 8)]
    for cp in t_z:
        cp.start()

    ld_weight.wait()
    bias_row = bias[...].astype(f32).reshape(1, CO)
    wflat = wv.reshape(9 * CI, CO)

    def conv(parts):
        lhs = jnp.concatenate(parts, axis=1)
        return jnp.dot(lhs, wflat[...], preferred_element_type=f32) + bias_row

    def taps(h, n):
        return [xs[b, h + a + 1 : h + a + 1 + n].reshape(n * TC, CI) for a in range(3) for b in range(3)]

    scale = 1.0 / math.sqrt(CO)

    def add_gram(feat, fresh):
        lo, hi = feat[:, 0:256], feat[:, 256:512]
        prods = [
            lax.dot_general(one, two, (((0,), (0,)), ((), ())), preferred_element_type=f32)
            for one, two in ((lo, lo), (lo, hi), (hi, hi))
        ]
        for q, side, rows, at in PANELS:
            part = prods[q][0:rows, side * 128 : side * 128 + 128]
            pan[at : at + rows] = part if fresh else pan[at : at + rows] + part

    feat, slope = gelu_pair(conv(taps(1, 6)))
    feats[2 * TC : 8 * TC] = feat.astype(bf16)
    deriv[2 * TC : 8 * TC] = slope * scale
    sub16 = lax.broadcasted_iota(jnp.int32, (16, CO), 0)

    def put_row(ref, at, place, row):
        old = ref[at : at + 16].astype(f32)
        ref[at : at + 16] = jnp.where(sub16 == place, row, old).astype(ref.dtype)

    for h in range(1, 7):
        put_row(feats, (h + 1) * TC, 0, 0.0)
        put_row(feats, (h + 2) * TC - 16, 15, 0.0)
    add_gram(feats[2 * TC : 8 * TC], True)

    each_halo(kinds[:8], lambda dr, dc, outer: halo_copy(-dr, -dc, outer).wait_recv())
    shift_row(1)
    shift_row(TR + 2)
    for i in range(1, TR + 3):
        shift_edges(i)
    first = xs[1, 1 : TR + 3, 0:8].astype(f32)
    last = xs[1, 1 : TR + 3, TC - 8 : TC].astype(f32)
    lcols = left[...].astype(f32)
    rcols = right[...].astype(f32)
    mid_l, mid_r = lcols[1 : TR + 3], rcols[1 : TR + 3]
    sides = ((mid_l[:, 7], first[:, 0], first[:, 1]), (last[:, 6], last[:, 7], mid_r[:, 0]))
    for s, cols in enumerate(sides):
        for b in range(3):
            for a in range(3):
                k = (a * 3 + b) * CI
                edgex[8 * s : 8 * s + 8, k : k + CI] = cols[b][a : a + 8]
    lhs = [
        jnp.concatenate([one, two, edgex[:, k * CI : k * CI + CI].astype(bf16)], axis=0)
        for k, (one, two) in enumerate(zip(taps(0, 1), taps(7, 1), strict=True))
    ]
    feat, slope = gelu_pair(conv(lhs))
    slope = slope * scale
    feats[TC : 2 * TC] = feat[0:TC].astype(bf16)
    deriv[TC : 2 * TC] = slope[0:TC]
    feats[8 * TC : 9 * TC] = feat[TC : 2 * TC].astype(bf16)
    deriv[8 * TC : 9 * TC] = slope[TC : 2 * TC]
    edge_f, edge_d = feat[2 * TC :], slope[2 * TC :]
    corner = jnp.logical_or(sub16 % 8 == 0, sub16 % 8 == 7)
    add_gram(jnp.concatenate([feat[0 : 2 * TC], jnp.where(corner, 0.0, edge_f)], axis=0).astype(bf16), False)

    own_half = pl.multiple_of(core * HALF, HALF)
    other_half = pl.multiple_of((1 - core) * HALF, HALF)
    s0[...] = pan[pl.ds(other_half, HALF)].astype(bf16)
    g_sib = rcopy(s0, r0, send.at[8], srecv, sib)
    g_sib.start()
    g_sib.wait_recv()
    both = pan[pl.ds(own_half, HALF)] + r0[...].astype(f32)
    s1[...] = both.astype(bf16)

    g_xy = [
        rcopy(s1.at[pl.ds(pl.multiple_of(CHUNK * xyk(j), 8), CHUNK)], r1.at[j], send.at[8 + j], xrecv.at[j], xyp(j))
        for j in range(1, 16)
    ]
    for cp in g_xy:
        cp.start()
    own_rows = pl.multiple_of(own_half + CHUNK * xy, 8)
    pan[pl.ds(own_half, HALF)] = both

    for h in range(1, 7):
        for s, (at, place) in enumerate((((h + 1) * TC, 0), ((h + 2) * TC - 16, 15))):
            put_row(feats, at, place, edge_f[8 * s + h : 8 * s + h + 1])
            put_row(deriv, at, place, edge_d[8 * s + h : 8 * s + h + 1])
    each_halo(kinds[8:], lambda dr, dc, outer: halo_copy(-dr, -dc, outer).wait_recv())
    for i in (0, TR + 3):
        shift_row(i)
        shift_edges(i)
    up_on = jnp.where(has_up, scale, 0.0).astype(f32)
    dn_on = jnp.where(has_dn, scale, 0.0).astype(f32)
    lf_on = jnp.where(has_lf, 1.0, 0.0).astype(f32)
    rt_on = jnp.where(has_rt, 1.0, 0.0).astype(f32)
    ringx[...] = jnp.zeros(ringx.shape, f32)
    first = xs[1, :, 0:8].astype(f32)
    last = xs[1, :, TC - 8 : TC].astype(f32)
    sides = ((lcols[:, 6], lcols[:, 7], first[:, 0]), (last[:, 7], rcols[:, 0], rcols[:, 1]))
    for s, cols in enumerate(sides):
        for b in range(3):
            for a in range(3):
                k = (a * 3 + b) * CI
                ringx[16 * s : 16 * s + 10, k : k + CI] = cols[b][a : a + 10]
    lhs = [
        jnp.concatenate([one, two, ringx[:, k * CI : k * CI + CI].astype(bf16)], axis=0)
        for k, (one, two) in enumerate(zip(taps(-1, 1), taps(8, 1), strict=True))
    ]
    feat, slope = gelu_pair(conv(lhs))
    feats[0:TC] = feat[0:TC].astype(bf16)
    deriv[0:TC] = slope[0:TC] * up_on
    feats[9 * TC : 10 * TC] = feat[TC : 2 * TC].astype(bf16)
    deriv[9 * TC : 10 * TC] = slope[TC : 2 * TC] * dn_on
    ring_row = lax.broadcasted_iota(jnp.int32, (32, CO), 0)
    side_on = jnp.where(ring_row < 16, lf_on, rt_on)
    pos = ring_row % 16
    row_on = jnp.where(pos == 0, up_on, jnp.where(pos == 9, dn_on, jnp.where(pos < 9, scale, 0.0)))
    feats[RING : RING + 32] = feat[2 * TC :].astype(bf16)
    deriv[RING : RING + 32] = slope[2 * TC :] * (side_on * row_on)

    for cp in t_z:
        cp.wait_recv()
    for zz in range(2):
        for b in range(2):
            rows16 = jnp.concatenate([tz[q * 2 + zz][b * 4 : b * 4 + 4] for q in range(4)], axis=0)
            tc[(zz * 2 + b) * 16 : (zz * 2 + b) * 16 + 16] = rows16.astype(bf16)
    own_t = tb.at[core, pl.ds(pl.multiple_of(64 * xy, 64), 64)]
    t_xy = [rcopy(tc, own_t, send.at[23 + j], txrecv.at[j], xyp(j)) for j in range(1, 16)]
    for cp in t_xy:
        cp.start()
    tb[core, pl.ds(pl.multiple_of(64 * xy, 64), 64)] = tc[...]

    acc = pan[pl.ds(own_rows, CHUNK)]
    for j in range(1, 16):
        g_xy[j - 1].wait_recv()
        acc = acc + r1[j].astype(f32)
    s2[...] = acc.astype(bf16)

    g_z = [rcopy(s2, r2.at[j], send.at[38 + j], zrecv.at[j], zp(j)) for j in range(1, 8)]
    for cp in g_z:
        cp.start()
    for a in range(3):
        for b in range(3):
            wt[a * CO : a * CO + CO, b * CI : b * CI + CI] = wv[3 * a + b].T
    acc = s2[...].astype(f32)
    for j in range(1, 8):
        g_z[j - 1].wait_recv()
        acc = acc + r2[j].astype(f32)
    s3[...] = (acc * (1.0 / NPIX)).astype(bf16)

    own_g = gf.at[pl.ds(own_rows, CHUNK)]
    for other in (1, 0):
        for j in range(1, 16):
            cross = 16 * jnp.where(core == other, 0, 1)
            dev = (zl * 16 + xyk(j), c - core + other)
            rcopy(s3, own_g, send.at[79 + 16 * other + j], arecv.at[cross + j], dev).start()
        if other == 1:
            g_own = rcopy(s3, own_g, send.at[79], arecv.at[16], sib)
            g_own.start()
            keep = pltpu.make_async_copy(s3, own_g, lsem.at[0])
            keep.start()

    for cp in t_xy:
        cp.wait_recv()
    t_fw = rcopy(tb.at[core], tb.at[core], send.at[63], tfrecv, sib)
    t_fw.start()
    t_fw.wait_recv()

    def tquad(i, k):
        halves = []
        for q in range(2):
            blk = tb[k].reshape(16, 4, 16, 128)[:, i * 2 + q].reshape(256, 128)
            halves.append(blk.astype(f32))
        return jnp.concatenate(halves, axis=1)

    t01 = tquad(0, 1) + tquad(1, 0).T
    t00 = tquad(0, 0)
    t11 = tquad(1, 1)
    tt[0] = t00 + t00.T
    tt[1] = t01
    tt[2] = t01.T
    tt[3] = t11 + t11.T

    keep.wait()
    for j in range(15, -1, -1):
        for cross in (0, 1):
            if j or cross:
                rcopy(s3, own_g, send.at[79], arecv.at[16 * cross + j], sib).wait_recv()

    def block(at):
        return gf[at : at + 128].astype(f32)

    def diagonal(at):
        cross = block(at + 128)
        top = jnp.concatenate([block(at), cross], axis=1)
        return jnp.concatenate([top, jnp.concatenate([cross.T, block(at + 256)], axis=1)], axis=0)

    g00, g11 = diagonal(0), diagonal(896)
    g01 = jnp.concatenate([gf[384:640], gf[640:896]], axis=1).astype(f32)
    g10 = g01.T
    sym[0:256, 0:256] = (2.0 * g00 - tt[0]).astype(bf16)
    sym[0:256, 256:512] = (2.0 * g01 - tt[1]).astype(bf16)
    sym[256:512, 0:256] = (2.0 * g10 - tt[2]).astype(bf16)
    sym[256:512, 256:512] = (2.0 * g11 - tt[3]).astype(bf16)
    gfull[0:256, 0:256] = g00
    gfull[0:256, 256:512] = g01
    gfull[256:512, 0:256] = g10
    gfull[256:512, 256:512] = g11

    for t in range(2):
        at = t * 5 * TC
        up = jnp.dot(feats[at : at + 5 * TC], sym[...], preferred_element_type=f32)
        gp[at : at + 5 * TC] = (up * deriv[at : at + 5 * TC]).astype(bf16)
    upr = jnp.dot(feats[RING : RING + 32], sym[...], preferred_element_type=f32)
    gring[...] = (upr * deriv[RING : RING + 32]).astype(bf16).astype(f32)

    for s, b in ((0, 2), (1, 0)):
        total = jnp.zeros((8, CI), f32)
        for a in range(3):
            rows8 = gring[16 * s + 2 - a : 16 * s + 10 - a].astype(bf16)
            total = total + jnp.dot(
                rows8, wt[a * CO : a * CO + CO, b * CI : b * CI + CI], preferred_element_type=f32
            )
        for h in range(TR):
            edge[s, h] = total[h : h + 1]

    for t in range(2):
        lhs = jnp.concatenate([gp[(4 * t + 2 - a) * TC : (4 * t + 6 - a) * TC] for a in range(3)], axis=1)
        total = jnp.dot(lhs, wt[...], preferred_element_type=f32)
        for i in range(4):
            h = 4 * t + i
            rows = total[i * TC : (i + 1) * TC]
            p0 = jnp.where(lane_row == TC - 1, edge[1, h], pltpu.roll(rows[:, 0:CI], TC - 1, axis=0))
            p2 = jnp.where(lane_row == 0, edge[0, h], pltpu.roll(rows[:, 2 * CI :], 1, axis=0))
            outv[h] = (rows[:, CI : 2 * CI] + p0 + p2).astype(bf16)

    own_row = zl * 256 + xy * 16 + zh * 4 + core * 2
    rows8 = gfull[pl.ds(pl.multiple_of((own_row // 8) * 8, 8), 8)]
    sub = lax.broadcasted_iota(jnp.int32, (8, CO), 0)
    for k in range(2):
        outg[k : k + 1] = jnp.sum(jnp.where(sub == own_row % 8 + k, rows8, 0.0), axis=0, keepdims=True)
    each_halo(kinds, lambda dr, dc, outer: halo_copy(dr, dc, outer).wait_send())
    for cp in [t_sib, g_sib, t_fw, g_own] + t_z + g_xy + t_xy + g_z:
        cp.wait_send()
    for other in (1, 0):
        for j in range(1, 16):
            rcopy(s3, own_g, send.at[79 + 16 * other + j], arecv.at[j], sib).wait_send()


def finish(gram, grad, gram_out, grad_out, sem):
    one = pltpu.make_async_copy(gram, gram_out, sem.at[0])
    two = pltpu.make_async_copy(grad, grad_out, sem.at[1])
    two.start()
    one.start()
    one.wait()
    two.wait()


def on_device(canvas, conv_weight, conv_bias, target_gram):
    hbm = pl.BlockSpec(memory_space=pl.ANY)
    vmem = pl.BlockSpec(memory_space=pltpu.VMEM)
    dma = pltpu.SemaphoreType.DMA
    held = (pltpu.VMEM((2, CO), f32), pltpu.VMEM((TR, TC, CI), bf16))
    shapes = (jax.ShapeDtypeStruct((2, CO), f32), jax.ShapeDtypeStruct((TR, TC, CI), bf16))
    gram, grad = pl.pallas_call(
        kernel,
        out_shape=held,
        in_specs=[hbm, hbm, vmem, hbm],
        out_specs=(vmem, vmem),
        scratch_shapes=[
            pltpu.VMEM((3, TR + 4, TC, CI), bf16),
            pltpu.VMEM((TR + 4, 8, CI), bf16),
            pltpu.VMEM((TR + 4, 8, CI), bf16),
            pltpu.VMEM((9, CI, CO), bf16),
            pltpu.VMEM((3 * CO, 3 * CI), bf16),
            pltpu.VMEM((RING + 32, CO), bf16),
            pltpu.VMEM((RING + 32, CO), f32),
            pltpu.VMEM((RING, CO), bf16),
            pltpu.VMEM((32, CO), f32),
            pltpu.VMEM((32, 9 * CI), f32),
            pltpu.VMEM((16, 9 * CI), f32),
            pltpu.VMEM((GROWS, 128), f32),
            pltpu.VMEM((HALF, 128), bf16),
            pltpu.VMEM((HALF, 128), bf16),
            pltpu.VMEM((HALF, 128), bf16),
            pltpu.VMEM((16, CHUNK, 128), bf16),
            pltpu.VMEM((CHUNK, 128), bf16),
            pltpu.VMEM((8, CHUNK, 128), bf16),
            pltpu.VMEM((CHUNK, 128), bf16),
            pltpu.VMEM((GROWS, 128), bf16),
            pltpu.VMEM((CO, CO), bf16),
            pltpu.VMEM((4, 256, 256), f32),
            pltpu.VMEM((CO, CO), f32),
            pltpu.VMEM((2, 2, CO), f32),
            pltpu.VMEM((8, 8, 128), f32),
            pltpu.VMEM((64, 128), bf16),
            pltpu.VMEM((2, 1024, 128), bf16),
            pltpu.VMEM((2, TR, 1, CI), f32),
            dma((3,)),
            dma((10,)),
            dma((10,)),
            dma((112,)),
            dma((16,)),
            dma((8,)),
            dma((32,)),
            dma,
            dma,
            dma((8,)),
            dma((16,)),
            dma,
        ],
        compiler_params=pltpu.CompilerParams(
            collective_id=0, has_side_effects=True, vmem_limit_bytes=56 * 1024 * 1024
        ),
        name="style_grad",
    )(canvas, conv_weight.reshape(9, CI, CO), conv_bias, target_gram)
    gram = pltpu.with_memory_space_constraint(gram, pltpu.VMEM)
    grad = pltpu.with_memory_space_constraint(grad, pltpu.VMEM)
    return pl.pallas_call(
        finish, out_shape=shapes, in_specs=[vmem, vmem], out_specs=(hbm, hbm), scratch_shapes=[dma((2,))], name="finish"
    )(gram, grad)


def solution(mesh):
    return jax.shard_map(
        on_device,
        mesh=mesh,
        in_specs=(P("rows", "cols", None), P(), P(), P(("rows", "cols"), None)),
        out_specs=(P(("rows", "cols"), None), P("rows", "cols", None)),
        check_vma=False,
    )
```
